512 devices in a mesh: sub: 32 (over z, core), mem: 16 (over x, y).
Axes of the slice: x: 4, y: 4, z: 16, core: 2. Of those that a mesh axis runs over, the one named last changes fastest.
Arguments:
- dechirped_echo_matrix: bfloat16 [32, 2, 256, 8192], P('sub', None, 'mem'), may hold values from -6 to 6
- bearing_rotation_table: float32 [32, 16, 512, 256], P('sub', 'mem'), may hold values from -3.140625 to 3.140625
- patch_subset_holder: int32 [32, 16, 16], P('sub', 'mem'), may hold values from 0 to 31, as said below
- modulation_slope: float32 [32, 16, 2, 16], P('sub', 'mem'), may hold values from -0.5 to 0.5
- regrid_lead_cell: int32 [32, 16, 2, 128], P('sub', 'mem'), may hold values from 0 to 124
- regrid_weight: float32 [32, 16, 2, 128], P('sub', 'mem'), may hold values from 0 to 1
Outputs:
- ground_image: bfloat16 [512, 2, 128, 128], P(('sub', 'mem'))
The draws below stay inside these ranges and needn't reach their ends.
Inputs may be any that keep to these rules, and one draw needn't show every extreme that they name: `patch_subset_holder`: each group and sector sends at most 2 of its 16 blocks to any one tile; in every sector some tile receives exactly 2 blocks from every group.
All inputs are finite; a program needn't handle non-finite values.
Results may differ from the reference program's by a relative error of at most 0.014.
Values may be sent and summed in bfloat16 or wider, within the bound.
No kernel may reach another device: no remote copies, remote signals or barrier semaphores. Data moves between devices by JAX's collectives and lax.ppermute only.
A program may use at most 64 MiB of HBM per device.

```python
import math
import jax
import jax.numpy as jnp
from jax import lax

FREQUENCIES = 8192
FIRST_RADIX = 64
SECOND_RADIX = 128
SWEEPS = 256
ANGLES = 512
BLOCK_SIDE = 128
LOOK_SUBSETS = 32
SLANT_DIVISIONS = 16
SECTOR_BINS = 512
TILT_PATCH_COUNT = 4
SLANT_PATCHES = 4
PATCHES_IN_SLICE = 16
CAPACITY = 2
TILES = 512


def draw_patch_subset_holder(key, part):
    full_key = jax.random.fold_in(key, 11)
    fullest = jax.random.randint(full_key, (SLANT_DIVISIONS,), 0, LOOK_SUBSETS, dtype=jnp.int32)
    targets = jnp.tile(fullest, LOOK_SUBSETS)
    numbers = jnp.arange(LOOK_SUBSETS * SLANT_DIVISIONS, dtype=jnp.int32) + 100
    seed_keys = jax.vmap(lambda number: jax.random.fold_in(key, number))(numbers)

    def one_device(seed_key, target):
        order_key = jax.random.fold_in(seed_key, 1)
        place_key = jax.random.fold_in(seed_key, 2)
        others = jnp.arange(LOOK_SUBSETS - 1, dtype=jnp.int32)
        others = others + (others >= target).astype(jnp.int32)
        pool_list = jnp.repeat(others, CAPACITY)
        pool_list = jax.random.permutation(order_key, pool_list)
        chosen = jnp.concatenate([jnp.full((CAPACITY,), target, dtype=jnp.int32), pool_list[:PATCHES_IN_SLICE - CAPACITY]])
        return jax.random.permutation(place_key, chosen)
    owners = jax.vmap(one_device)(seed_keys, targets)
    return owners.reshape(LOOK_SUBSETS, SLANT_DIVISIONS, PATCHES_IN_SLICE).astype(jnp.int32)


def plant(drawn, stream_key, smallest, top_value):
    place = [jax.random.randint(jax.random.fold_in(stream_key, axis), (), 0, length) for axis, length in enumerate(drawn.shape)]
    longest = drawn.shape.index(max(drawn.shape))
    neighbour = place[:longest] + [(place[longest] + 1) % drawn.shape[longest]] + place[longest + 1:]
    return drawn.at[tuple(place)].set(smallest).at[tuple(neighbour)].set(top_value)


def block_scale(rng, dims, split, least, top_value):
    def one(position, parts):
        draws = jax.random.uniform(jax.random.fold_in(jax.random.fold_in(rng, 6), position), (parts,), jnp.float32, least / len(split), top_value / len(split))
        return jnp.repeat(jnp.exp(draws), dims[position] // parts).reshape((-1,) + (1,) * (len(dims) - position - 1))

    gain = one(*split[0])
    for cut in split[1:]:
        gain = gain * one(*cut)
    return gain


def bell_draw(stream_key, dims, width, most, pieces=(), kind=jnp.bfloat16):
    factor_of = block_scale(stream_key, dims, pieces, -0.22, 0.18) if pieces else 1.0
    result = jax.random.normal(stream_key, dims, jnp.float32) * width * factor_of
    return jnp.minimum(jnp.maximum(result, -most), most).astype(kind)


def setup_inputs(seed: int = 0) -> dict:
    key_list = jax.random.split(jax.random.key(seed), 7)
    dechirped_echo_matrix = bell_draw(key_list[0], (LOOK_SUBSETS, 2, SWEEPS, FREQUENCIES), 1.0, 6.0, ((0, 32), (2, 16)))
    bearing_rotation_table = jnp.clip(jax.random.uniform(key_list[1], (LOOK_SUBSETS, SLANT_DIVISIONS, ANGLES, SWEEPS), jnp.float32, -3.140625, 3.140625), -3.140625, 3.140625)
    patch_subset_holder = draw_patch_subset_holder(jax.random.fold_in(key_list[6], 71), 0)
    modulation_slope = jnp.clip(jax.random.uniform(key_list[3], (LOOK_SUBSETS, SLANT_DIVISIONS, 2, PATCHES_IN_SLICE), jnp.float32, -0.5, 0.5) * block_scale(key_list[3], (LOOK_SUBSETS, SLANT_DIVISIONS, 2, PATCHES_IN_SLICE), ((0, 32), (1, 16)), -0.4, 0.0), -0.5, 0.5)
    regrid_lead_cell = plant(jax.random.randint(key_list[4], (LOOK_SUBSETS, SLANT_DIVISIONS, 2, BLOCK_SIDE), 0, BLOCK_SIDE - 3), jax.random.fold_in(key_list[4], 1), 0, (BLOCK_SIDE - 3) - 1).astype(jnp.int32)
    regrid_weight = jnp.clip(1.0 * jax.random.uniform(key_list[5], (LOOK_SUBSETS, SLANT_DIVISIONS, 2, BLOCK_SIDE), jnp.float32) ** block_scale(key_list[5], (LOOK_SUBSETS, SLANT_DIVISIONS, 2, BLOCK_SIDE), ((0, 32), (1, 16)), -0.2, 0.2), 0.0, 1.0)
    return dict(dechirped_echo_matrix=dechirped_echo_matrix, bearing_rotation_table=bearing_rotation_table, patch_subset_holder=patch_subset_holder, modulation_slope=modulation_slope, regrid_lead_cell=regrid_lead_cell, regrid_weight=regrid_weight)


def dft_tables(length):
    positions = jnp.arange(length, dtype=jnp.int32)
    turns = positions[:, None] * positions[None, :] % length
    phase_angle = turns.astype(jnp.float32) * (2.0 * math.pi / length)
    return jnp.stack([jnp.cos(phase_angle), jnp.sin(phase_angle)]).astype(jnp.bfloat16)

def twiddle(row_count, column_count, length):
    row_index = jnp.arange(row_count, dtype=jnp.int32)
    column_index = jnp.arange(column_count, dtype=jnp.int32)
    turns = row_index[:, None] * column_index[None, :] % length
    phase_angle = turns.astype(jnp.float32) * (2.0 * math.pi / length)
    return (jnp.cos(phase_angle), jnp.sin(phase_angle))

def combine(product):
    return (product[0, 0] - product[1, 1], product[0, 1] + product[1, 0])

def range_transform(sweeps):
    sweep_count = sweeps.shape[1]
    reshaped = sweeps.reshape(2, sweep_count, FIRST_RADIX, SECOND_RADIX).astype(jnp.float32)
    product = jnp.einsum('qrk,pskj->qpsrj', dft_tables(FIRST_RADIX).astype(jnp.float32), reshaped)
    inphase_part, quadrature_part = combine(product)
    cosine, sine_part = twiddle(FIRST_RADIX, SECOND_RADIX, FREQUENCIES)
    turned = jnp.stack([inphase_part * cosine - quadrature_part * sine_part, inphase_part * sine_part + quadrature_part * cosine]).astype(jnp.bfloat16)
    product = jnp.einsum('quj,psrj->qpsur', dft_tables(SECOND_RADIX).astype(jnp.float32), turned.astype(jnp.float32))
    inphase_part, quadrature_part = combine(product)
    factor = 1.0 / math.sqrt(FREQUENCIES)
    return (jnp.stack([inphase_part, quadrature_part]) * factor).astype(jnp.bfloat16).reshape(2, sweep_count, FREQUENCIES)

def phase_tables(angles):
    factor = 1.0 / math.sqrt(SWEEPS)
    return jnp.stack([jnp.cos(angles) * factor, jnp.sin(angles) * factor]).astype(jnp.bfloat16)

def strip_modulation(inphase_part, quadrature_part, modulation_line_entries):
    tilt_linear_slope = modulation_line_entries[0].reshape(TILT_PATCH_COUNT, SLANT_PATCHES)
    slant_linear_slope = modulation_line_entries[1].reshape(TILT_PATCH_COUNT, SLANT_PATCHES)
    positions = jnp.arange(BLOCK_SIDE, dtype=jnp.float32)
    phase_angle = tilt_linear_slope[:, None, :, None] * positions[None, :, None, None] + slant_linear_slope[:, None, :, None] * positions[None, None, None, :]
    cosine = jnp.cos(phase_angle)
    sine_part = jnp.sin(phase_angle)
    inphase_part = inphase_part.reshape(TILT_PATCH_COUNT, BLOCK_SIDE, SLANT_PATCHES, BLOCK_SIDE)
    quadrature_part = quadrature_part.reshape(TILT_PATCH_COUNT, BLOCK_SIDE, SLANT_PATCHES, BLOCK_SIDE)
    return jnp.stack([inphase_part * cosine - quadrature_part * sine_part, inphase_part * sine_part + quadrature_part * cosine]).astype(jnp.bfloat16)

def stencil(offsets, fractions):
    shift_part = fractions
    weights = [-shift_part * (shift_part - 1.0) * (shift_part - 2.0) / 6.0, (shift_part + 1.0) * (shift_part - 1.0) * (shift_part - 2.0) / 2.0, -(shift_part + 1.0) * shift_part * (shift_part - 2.0) / 2.0, (shift_part + 1.0) * shift_part * (shift_part - 1.0) / 6.0]
    sources = jnp.arange(fractions.shape[-1], dtype=jnp.int32)
    distance = sources - offsets[..., None]
    weights_sum = jnp.zeros(distance.shape, jnp.float32)
    for stencil_tap in range(4):
        weights_sum = weights_sum + jnp.where(distance == stencil_tap, weights[stencil_tap][..., None], jnp.float32(0.0))
    return weights_sum.astype(jnp.bfloat16)

def reference(dechirped_echo_matrix, bearing_rotation_table, patch_subset_holder, modulation_slope, regrid_lead_cell, regrid_weight):
    tables_all = stencil(regrid_lead_cell, regrid_weight).reshape(TILES, 2, BLOCK_SIDE, BLOCK_SIDE)
    sector_rows = jnp.arange(SLANT_DIVISIONS, dtype=jnp.int32)

    def lone_subset(picture_buffer, inputs):
        history, angles, owners, linear_slopes = inputs
        spectrum = range_transform(history)
        by_sector = spectrum.reshape(2, SWEEPS, SLANT_DIVISIONS, SECTOR_BINS).astype(jnp.float32)
        product = jnp.einsum('qmas,psmc->qpmac', phase_tables(angles).astype(jnp.float32), by_sector)
        inphase_part, quadrature_part = combine(product)
        patch_list = jax.vmap(strip_modulation)(inphase_part, quadrature_part, linear_slopes)
        tile_index = (owners * SLANT_DIVISIONS + sector_rows[:, None]).astype(jnp.int32)
        chosen = tables_all[tile_index.reshape(-1)].reshape(SLANT_DIVISIONS, TILT_PATCH_COUNT, SLANT_PATCHES, 2, BLOCK_SIDE, BLOCK_SIDE).astype(jnp.float32)
        rows_done = jnp.einsum('mACya,mpAaCc->mACpyc', chosen[:, :, :, 0], patch_list.astype(jnp.float32)).astype(jnp.bfloat16)
        interpolated = jnp.einsum('mACpyc,mACxc->mACpyx', rows_done.astype(jnp.float32), chosen[:, :, :, 1])
        partial_sum = jax.ops.segment_sum(interpolated.reshape(-1, 2, BLOCK_SIDE, BLOCK_SIDE), tile_index.reshape(-1), num_segments=TILES)
        rounded = lax.optimization_barrier(partial_sum.astype(jnp.bfloat16)).astype(jnp.float32)
        return (picture_buffer + rounded, None)
    initial_location = jnp.zeros((TILES, 2, BLOCK_SIDE, BLOCK_SIDE), jnp.float32)
    picture_buffer, discarded_entry = lax.scan(lone_subset, initial_location, (dechirped_echo_matrix, bearing_rotation_table, patch_subset_holder, modulation_slope))
    return (0.25 * picture_buffer).astype(jnp.bfloat16)
```

```python
import functools
import math

import jax
import jax.numpy as jnp
from jax import lax
from jax.experimental import pallas as pl
from jax.experimental.pallas import tpu as pltpu
from jax.sharding import PartitionSpec as P

FREQUENCIES = 8192
FIRST_RADIX = 64
SECOND_RADIX = 128
SWEEPS = 256
ANGLES = 512
BLOCK_SIDE = 128
F32 = jnp.float32
BF16 = jnp.bfloat16


def dft_tables(length):
    positions = jnp.arange(length, dtype=jnp.int32)
    turns = positions[:, None] * positions[None, :] % length
    phase_angle = turns.astype(F32) * (2.0 * math.pi / length)
    return jnp.stack([jnp.cos(phase_angle), jnp.sin(phase_angle)]).astype(BF16)


def twiddle(row_count, column_count, length):
    row_index = jnp.arange(row_count, dtype=jnp.int32)
    column_index = jnp.arange(column_count, dtype=jnp.int32)
    turns = row_index[:, None] * column_index[None, :] % length
    phase_angle = turns.astype(F32) * (2.0 * math.pi / length)
    return (jnp.cos(phase_angle), jnp.sin(phase_angle))


def combine(product):
    return (product[0, 0] - product[1, 1], product[0, 1] + product[1, 0])


def range_transform(sweeps):
    sweep_count = sweeps.shape[1]
    reshaped = sweeps.reshape(2, sweep_count, FIRST_RADIX, SECOND_RADIX)
    product = jnp.einsum(
        "qrk,pskj->qpsrj", dft_tables(FIRST_RADIX), reshaped, preferred_element_type=F32
    )
    inphase_part, quadrature_part = combine(product)
    cosine, sine_part = twiddle(FIRST_RADIX, SECOND_RADIX, FREQUENCIES)
    turned = jnp.stack(
        [
            inphase_part * cosine - quadrature_part * sine_part,
            inphase_part * sine_part + quadrature_part * cosine,
        ]
    ).astype(BF16)
    product = jnp.einsum(
        "quj,psrj->qpsur", dft_tables(SECOND_RADIX), turned, preferred_element_type=F32
    )
    inphase_part, quadrature_part = combine(product)
    factor = 1.0 / math.sqrt(FREQUENCIES)
    return (
        (jnp.stack([inphase_part, quadrature_part]) * factor)
        .astype(BF16)
        .reshape(2, sweep_count, FREQUENCIES)
    )


def phase_tables(angles):
    factor = 1.0 / math.sqrt(SWEEPS)
    return jnp.stack([jnp.cos(angles) * factor, jnp.sin(angles) * factor]).astype(BF16)


def stencil(offsets, fractions):
    weights = [
        -fractions * (fractions - 1.0) * (fractions - 2.0) / 6.0,
        (fractions + 1.0) * (fractions - 1.0) * (fractions - 2.0) / 2.0,
        -(fractions + 1.0) * fractions * (fractions - 2.0) / 2.0,
        (fractions + 1.0) * fractions * (fractions - 1.0) / 6.0,
    ]
    sources = jnp.arange(fractions.shape[-1], dtype=jnp.int32)
    distance = sources - offsets[..., None]
    weights_sum = jnp.zeros(distance.shape, F32)
    for stencil_tap in range(4):
        weights_sum = weights_sum + jnp.where(
            distance == stencil_tap, weights[stencil_tap][..., None], F32(0.0)
        )
    return weights_sum.astype(BF16)


def focus_kernel(slots, tab, z, cu, su, cv, sv, own, other):
    half = own.shape[1]
    own[...] = jnp.zeros_like(own)
    other[...] = jnp.zeros_like(other)
    side = BLOCK_SIDE
    sector = z.shape[-1]
    rows = z.shape[0] * z.shape[2]
    zre = z[:, 0].reshape(rows, sector)
    zim = z[:, 1].reshape(rows, sector)
    for ab in range(tab.shape[1] // side):
        span = slice(ab * side, (ab + 1) * side)
        pc = tab[0, span, :]
        ps = tab[1, span, :]
        dot = functools.partial(jnp.dot, preferred_element_type=F32)
        re = dot(pc, zre) - dot(ps, zim)
        im = dot(pc, zim) + dot(ps, zre)
        for cb in range(sector // side):
            lanes = slice(cb * side, (cb + 1) * side)
            c0 = cu[span, cb : cb + 1]
            s0 = su[span, cb : cb + 1]
            c1 = cv[ab : ab + 1, lanes]
            s1 = sv[ab : ab + 1, lanes]
            cosine = c0 * c1 - s0 * s1
            sine = s0 * c1 + c0 * s1
            r, i = re[:, lanes], im[:, lanes]
            dre = (r * cosine - i * sine).astype(BF16).astype(F32)
            dim = (r * sine + i * cosine).astype(BF16).astype(F32)
            slot = slots[ab * (sector // side) + cb]

            def add(ref, index):
                ref[0, index] = (ref[0, index].astype(F32) + dre).astype(BF16)
                ref[1, index] = (ref[1, index].astype(F32) + dim).astype(BF16)

            @pl.when(slot < half)
            def _():
                add(own, slot)

            @pl.when(slot >= half)
            def _():
                add(other, slot - half)


def focus(slots, tab, z, cu, su, cv, sv, half):
    shape = jax.ShapeDtypeStruct((2, half, BLOCK_SIDE, BLOCK_SIDE), BF16)
    vmem = pl.BlockSpec(memory_space=pltpu.VMEM)
    return pl.pallas_call(
        focus_kernel,
        out_shape=(shape, shape),
        in_specs=[pl.BlockSpec(memory_space=pltpu.SMEM)] + [vmem] * 6,
        out_specs=(vmem, vmem),
        name="focus",
    )(slots, tab, z, cu, su, cv, sv)


def on_device(
    dechirped_echo_matrix,
    bearing_rotation_table,
    patch_subset_holder,
    modulation_slope,
    regrid_lead_cell,
    regrid_weight,
):
    groups = lax.axis_size("sub")
    members = lax.axis_size("mem")
    chips = groups // 2
    sector = FREQUENCIES // members
    ab_count = ANGLES // BLOCK_SIDE
    cb_count = sector // BLOCK_SIDE

    spectrum = range_transform(dechirped_echo_matrix[0])
    sweep_count = spectrum.shape[1]
    by_sector = spectrum.reshape(2, sweep_count, members, sector).transpose(2, 0, 1, 3)
    z = lax.all_to_all(by_sector, "mem", split_axis=0, concat_axis=0, tiled=True)

    tables = phase_tables(bearing_rotation_table[0, 0])
    positions = jnp.arange(BLOCK_SIDE, dtype=F32)
    slope = modulation_slope[0, 0].reshape(2, ab_count, cb_count)
    u_phase = (slope[0][:, None, :] * positions[None, :, None]).reshape(ANGLES, cb_count)
    v_phase = (slope[1][:, :, None] * positions[None, None, :]).reshape(ab_count, sector)

    me = lax.axis_index("sub")
    owners = patch_subset_holder[0, 0]
    apart = owners ^ me
    slots = (apart & 1) * chips + ((apart >> 1) & 1) * (chips // 2) + (owners >> 2)

    own, other = focus(
        slots, tables, z, jnp.cos(u_phase), jnp.sin(u_phase), jnp.cos(v_phase), jnp.sin(v_phase), chips
    )
    core_swap = [(i, i ^ 1) for i in range(groups)]
    held = own + lax.ppermute(other, "sub", core_swap)

    def partner(z, shift):
        w = z + shift
        return ((w ^ 1) - shift) % chips

    def pairing(shift):
        return [(2 * z + c, 2 * partner(z, shift) + c) for z in range(chips) for c in range(2)]

    kept = chips // 2
    first = held[0, :kept] + lax.ppermute(held[0, kept:], "sub", pairing(0))
    second = held[1, :kept] + lax.ppermute(held[1, kept:], "sub", pairing(1))
    alike = [[2 * z + c for z in range(par, chips, 2)] for par in range(2) for c in range(2)]
    arrived = lax.all_to_all(
        jnp.stack([first, second], axis=1),
        "sub",
        split_axis=0,
        concat_axis=0,
        tiled=True,
        axis_index_groups=alike,
    )
    gathered = jnp.sum(arrived.astype(F32), axis=0).astype(BF16)
    own_tables = stencil(regrid_lead_cell[0, 0], regrid_weight[0, 0])
    rows_done = jnp.einsum(
        "ya,pac->pyc", own_tables[0], gathered, preferred_element_type=F32
    ).astype(BF16)
    ground = jnp.einsum("pyc,xc->pyx", rows_done, own_tables[1], preferred_element_type=F32)
    return (0.25 * ground).astype(BF16)[None]


def solution(mesh):
    return jax.shard_map(
        on_device,
        mesh=mesh,
        in_specs=(
            P("sub", None, "mem", None),
            P("sub", "mem", None, None),
            P("sub", "mem", None),
            P("sub", "mem", None, None),
            P("sub", "mem", None, None),
            P("sub", "mem", None, None),
        ),
        out_specs=P(("sub", "mem"), None, None, None),
        check_vma=False,
    )
```

```python
import functools
import math

import jax
import jax.numpy as jnp
from jax import lax
from jax.experimental import pallas as pl
from jax.experimental.pallas import tpu as pltpu
from jax.sharding import PartitionSpec as P

FREQUENCIES = 8192
FIRST_RADIX = 64
SECOND_RADIX = 128
SWEEPS = 256
ANGLES = 512
BLOCK_SIDE = 128
F32 = jnp.float32
BF16 = jnp.bfloat16


def dft_tables(length):
    positions = jnp.arange(length, dtype=jnp.int32)
    turns = positions[:, None] * positions[None, :] % length
    phase_angle = turns.astype(F32) * (2.0 * math.pi / length)
    return jnp.stack([jnp.cos(phase_angle), jnp.sin(phase_angle)]).astype(BF16)


def twiddle(row_count, column_count, length):
    row_index = jnp.arange(row_count, dtype=jnp.int32)
    column_index = jnp.arange(column_count, dtype=jnp.int32)
    turns = row_index[:, None] * column_index[None, :] % length
    phase_angle = turns.astype(F32) * (2.0 * math.pi / length)
    return (jnp.cos(phase_angle), jnp.sin(phase_angle))


def combine(product):
    return (product[0, 0] - product[1, 1], product[0, 1] + product[1, 0])


def range_transform(sweeps):
    sweep_count = sweeps.shape[1]
    reshaped = sweeps.reshape(2, sweep_count, FIRST_RADIX, SECOND_RADIX)
    product = jnp.einsum(
        "qrk,pskj->qpsrj", dft_tables(FIRST_RADIX), reshaped, preferred_element_type=F32
    )
    inphase_part, quadrature_part = combine(product)
    cosine, sine_part = twiddle(FIRST_RADIX, SECOND_RADIX, FREQUENCIES)
    turned = jnp.stack(
        [
            inphase_part * cosine - quadrature_part * sine_part,
            inphase_part * sine_part + quadrature_part * cosine,
        ]
    ).astype(BF16)
    product = jnp.einsum(
        "quj,psrj->qpsur", dft_tables(SECOND_RADIX), turned, preferred_element_type=F32
    )
    inphase_part, quadrature_part = combine(product)
    factor = 1.0 / math.sqrt(FREQUENCIES)
    return (
        (jnp.stack([inphase_part, quadrature_part]) * factor)
        .astype(BF16)
        .reshape(2, sweep_count, FREQUENCIES)
    )


def phase_tables(angles):
    factor = 1.0 / math.sqrt(SWEEPS)
    return jnp.concatenate([jnp.cos(angles) * factor, jnp.sin(angles) * factor], axis=1).astype(BF16)


def stencil(offsets, fractions):
    weights = [
        -fractions * (fractions - 1.0) * (fractions - 2.0) / 6.0,
        (fractions + 1.0) * (fractions - 1.0) * (fractions - 2.0) / 2.0,
        -(fractions + 1.0) * fractions * (fractions - 2.0) / 2.0,
        (fractions + 1.0) * fractions * (fractions - 1.0) / 6.0,
    ]
    sources = jnp.arange(fractions.shape[-1], dtype=jnp.int32)
    distance = sources - offsets[..., None]
    weights_sum = jnp.zeros(distance.shape, F32)
    for stencil_tap in range(4):
        weights_sum = weights_sum + jnp.where(
            distance == stencil_tap, weights[stencil_tap][..., None], F32(0.0)
        )
    return weights_sum.astype(BF16)


def focus_kernel(row, owners, tab, z, cosines, sines, own, other):
    half = own.shape[0]
    own[...] = jnp.zeros_like(own)
    other[...] = jnp.zeros_like(other)
    side = BLOCK_SIDE
    height = own.shape[2]
    sector = z.shape[-1]
    cb_count = sector // side
    rows = z.shape[0] * z.shape[2]
    me = owners[0, owners.shape[1] - 1]
    zre = z[:, 0].reshape(rows, sector)
    zim = z[:, 1].reshape(rows, sector)
    dot = functools.partial(jnp.dot, preferred_element_type=F32)
    into_re = jnp.concatenate([zre, -zim], axis=0)
    into_im = jnp.concatenate([zim, zre], axis=0)
    for ab in range(tab.shape[0] // height):
        span = slice(ab * height, (ab + 1) * height)
        re = dot(tab[span, :], into_re)
        im = dot(tab[span, :], into_im)
        lines = slice(ab * side, (ab + 1) * side)
        cu = cosines[:, lines].T[row : row + height]
        su = sines[:, lines].T[row : row + height]
        for cb in range(cb_count):
            lanes = slice(cb * side, (cb + 1) * side)
            c0, s0 = cu[:, cb : cb + 1], su[:, cb : cb + 1]
            c1 = cosines[cb_count + ab : cb_count + ab + 1, lanes]
            s1 = sines[cb_count + ab : cb_count + ab + 1, lanes]
            cosine = c0 * c1 - s0 * s1
            sine = s0 * c1 + c0 * s1
            r, i = re[:, lanes], im[:, lanes]
            dre = (r * cosine - i * sine).astype(BF16).astype(F32)
            dim = (r * sine + i * cosine).astype(BF16).astype(F32)
            owner = owners[0, ab * cb_count + cb]
            apart = owner ^ me
            index = ((apart >> 1) & 1) * (half // 2) + (owner >> 2)

            def add(ref):
                ref[index, 0] = (ref[index, 0].astype(F32) + dre).astype(BF16)
                ref[index, 1] = (ref[index, 1].astype(F32) + dim).astype(BF16)

            @pl.when((apart & 1) == 0)
            def _():
                add(own)

            @pl.when((apart & 1) == 1)
            def _():
                add(other)


def focus(part, owners, tab, z, cosines, sines, slots):
    height = BLOCK_SIDE // 2
    shape = pltpu.VMEM((slots, 2, height, BLOCK_SIDE), BF16)
    vmem = pl.BlockSpec(memory_space=pltpu.VMEM)
    return pl.pallas_call(
        functools.partial(focus_kernel, part * height),
        out_shape=(shape, shape),
        in_specs=[pl.BlockSpec(memory_space=pltpu.SMEM)] + [vmem] * 4,
        out_specs=(vmem, vmem),
        name="focus",
    )(owners, *(pltpu.with_memory_space_constraint(x, pltpu.VMEM) for x in (tab, z, cosines, sines)))


def on_device(
    dechirped_echo_matrix,
    bearing_rotation_table,
    patch_subset_holder,
    modulation_slope,
    regrid_lead_cell,
    regrid_weight,
):
    groups = lax.axis_size("sub")
    members = lax.axis_size("mem")
    chips = groups // 2
    sector = FREQUENCIES // members
    ab_count = ANGLES // BLOCK_SIDE
    cb_count = sector // BLOCK_SIDE

    spectrum = range_transform(dechirped_echo_matrix[0])
    sweep_count = spectrum.shape[1]
    by_sector = spectrum.reshape(2, sweep_count, members, sector).transpose(2, 0, 1, 3)
    z = lax.all_to_all(by_sector, "mem", split_axis=0, concat_axis=0, tiled=True)

    height = BLOCK_SIDE // 2
    angles = bearing_rotation_table[0, 0].reshape(ab_count, 2, height, SWEEPS)
    tables = [phase_tables(angles[:, part].reshape(ANGLES // 2, SWEEPS)) for part in range(2)]
    positions = jnp.arange(BLOCK_SIDE, dtype=F32)
    slope = modulation_slope[0, 0].reshape(2, ab_count, cb_count)
    u_phase = slope[0].T[:, :, None] * positions
    v_phase = slope[1][:, :, None] * positions
    phase = jnp.concatenate([u_phase, v_phase]).reshape(cb_count + ab_count, sector)
    cosines, sines = jnp.cos(phase), jnp.sin(phase)

    me = lax.axis_index("sub").astype(jnp.int32)
    owners = jnp.concatenate([patch_subset_holder[0], me.reshape(1, 1)], axis=1)
    core_swap = [(i, i ^ 1) for i in range(groups)]

    def pairing(shift):
        partner = lambda z: (((z + shift) ^ 1) - shift) % chips
        return [(2 * z + c, 2 * partner(z) + c) for z in range(chips) for c in range(2)]

    kept = chips // 2
    parts = []
    for part in range(2):
        own, other = focus(part, owners, tables[part], z, cosines, sines, chips)
        held = own + lax.ppermute(other, "sub", core_swap)
        parts.append(held[:kept] + lax.ppermute(held[kept:], "sub", pairing(part)))
    alike = [[2 * z + c for z in range(par, chips, 2)] for par in range(2) for c in range(2)]
    arrived = lax.all_to_all(
        jnp.stack(parts, axis=1),
        "sub",
        split_axis=0,
        concat_axis=0,
        tiled=True,
        axis_index_groups=alike,
    )
    gathered = jnp.sum(arrived.astype(F32), axis=0).astype(BF16)
    gathered = gathered.transpose(1, 0, 2, 3).reshape(2, BLOCK_SIDE, BLOCK_SIDE)
    own_tables = stencil(regrid_lead_cell[0, 0], regrid_weight[0, 0])
    rows_done = jnp.einsum(
        "ya,pac->pyc", own_tables[0], gathered, preferred_element_type=F32
    ).astype(BF16)
    ground = jnp.einsum("pyc,xc->pyx", rows_done, own_tables[1], preferred_element_type=F32)
    return (0.25 * ground).astype(BF16)[None]


def solution(mesh):
    return jax.shard_map(
        on_device,
        mesh=mesh,
        in_specs=(
            P("sub", None, "mem", None),
            P("sub", "mem", None, None),
            P("sub", "mem", None),
            P("sub", "mem", None, None),
            P("sub", "mem", None, None),
            P("sub", "mem", None, None),
        ),
        out_specs=P(("sub", "mem"), None, None, None),
        check_vma=False,
    )
```

```python
import functools
import math

import jax
import jax.numpy as jnp
import numpy as np
from jax import lax
from jax.experimental import pallas as pl
from jax.experimental.pallas import tpu as pltpu
from jax.sharding import PartitionSpec as P

FREQUENCIES = 8192
FIRST_RADIX = 64
SECOND_RADIX = 128
SWEEPS = 256
ANGLES = 512
BLOCK_SIDE = 128
F32 = jnp.float32
BF16 = jnp.bfloat16


def range_constants():
    def table(length, rows):
        turns = np.outer(rows, np.arange(length)) % length
        angle = turns * (2.0 * np.pi / length)
        c, s = np.cos(angle), np.sin(angle)
        return np.concatenate([c, -s], axis=1), np.concatenate([s, c], axis=1)

    first = np.concatenate(table(FIRST_RADIX, np.arange(FIRST_RADIX)))
    second = np.concatenate(
        [part for odd in range(2) for part in table(SECOND_RADIX, np.arange(odd, SECOND_RADIX, 2))]
    )
    turns = np.outer(np.arange(FIRST_RADIX), np.arange(SECOND_RADIX)) % FREQUENCIES
    angle = turns * (2.0 * np.pi / FREQUENCIES)
    return (
        jnp.asarray(first.astype(np.float32)).astype(BF16),
        jnp.asarray(second.astype(np.float32)).astype(BF16),
        jnp.asarray(np.stack([np.cos(angle), np.sin(angle)]).astype(np.float32)),
    )


def range_kernel(x, first, second, turn, out, rows, turned, moved):
    sweeps = x.shape[1]
    lanes = SECOND_RADIX
    height = 2 * FIRST_RADIX
    for p in range(2):
        for k2 in range(FIRST_RADIX):
            tile = x[p, :, k2 * lanes : (k2 + 1) * lanes].astype(F32)
            rows[pl.ds(p * FIRST_RADIX + k2, sweeps, stride=height), :] = tile
    cosine, sine = turn[0], turn[1]
    for s in range(0, sweeps, 2):
        pair = [rows[(s + i) * height : (s + i + 1) * height, :].astype(BF16) for i in range(2)]
        product = jnp.dot(first[...], jnp.concatenate(pair, axis=1), preferred_element_type=F32)
        for i in range(2):
            re = product[:FIRST_RADIX, i * lanes : (i + 1) * lanes]
            im = product[FIRST_RADIX:, i * lanes : (i + 1) * lanes]
            span = slice((s + i) * FIRST_RADIX, (s + i + 1) * FIRST_RADIX)
            turned[span, :lanes] = (re * cosine - im * sine).astype(BF16)
            turned[span, lanes:] = (re * sine + im * cosine).astype(BF16)
    factor = 1.0 / math.sqrt(FREQUENCIES)
    low = lax.broadcasted_iota(jnp.int32, (lanes, lanes), 1) < FIRST_RADIX
    for s in range(0, sweeps, 2):
        span = slice(s * FIRST_RADIX, (s + 2) * FIRST_RADIX)
        product = factor * lax.dot_general(
            second[...], turned[span, :], (((1,), (1,)), ((), ())), preferred_element_type=F32
        )
        even, odd = product[:lanes], product[lanes:]
        here = jnp.where(low, even, pltpu.roll(odd, FIRST_RADIX, 1))
        after = jnp.where(low, pltpu.roll(even, FIRST_RADIX, 1), odd)
        moved[pl.ds(s, lanes, stride=sweeps), :] = here
        moved[pl.ds(s + 1, lanes, stride=sweeps), :] = after
    members = out.shape[0]
    cb_count = out.shape[3] // lanes
    for q in range(2):
        for m in range(members):
            for cb in range(cb_count):
                row = ((q * members + m) * cb_count + cb) * sweeps
                out[m, q, :, cb * lanes : (cb + 1) * lanes] = moved[row : row + sweeps, :].astype(BF16)


def range_messages(sweeps, members):
    count = sweeps.shape[1]
    vmem = pl.BlockSpec(memory_space=pltpu.VMEM)
    return pl.pallas_call(
        range_kernel,
        out_shape=jax.ShapeDtypeStruct((members, 2, count, FREQUENCIES // members), BF16),
        in_specs=[vmem] * 4,
        out_specs=vmem,
        scratch_shapes=[
            pltpu.VMEM((count * 2 * FIRST_RADIX, SECOND_RADIX), F32),
            pltpu.VMEM((count * FIRST_RADIX, 2 * SECOND_RADIX), BF16),
            pltpu.VMEM((count * 2 * FIRST_RADIX, SECOND_RADIX), F32),
        ],
        name="range_transform",
    )(sweeps, *range_constants())


def phase_tables(angles):
    factor = 1.0 / math.sqrt(SWEEPS)
    return jnp.concatenate([jnp.cos(angles) * factor, jnp.sin(angles) * factor], axis=1).astype(BF16)


def stencil(offsets, fractions):
    weights = [
        -fractions * (fractions - 1.0) * (fractions - 2.0) / 6.0,
        (fractions + 1.0) * (fractions - 1.0) * (fractions - 2.0) / 2.0,
        -(fractions + 1.0) * fractions * (fractions - 2.0) / 2.0,
        (fractions + 1.0) * fractions * (fractions - 1.0) / 6.0,
    ]
    sources = jnp.arange(fractions.shape[-1], dtype=jnp.int32)
    distance = sources - offsets[..., None]
    weights_sum = jnp.zeros(distance.shape, F32)
    for stencil_tap in range(4):
        weights_sum = weights_sum + jnp.where(
            distance == stencil_tap, weights[stencil_tap][..., None], F32(0.0)
        )
    return weights_sum.astype(BF16)


def focus_kernel(row, owners, tab, z, cosines, sines, own, other, clean, sums):
    side = BLOCK_SIDE
    height = own.shape[2]
    sector = z.shape[-1]
    cb_count = sector // side
    rows = z.shape[0] * z.shape[2]
    zre = z[:, 0].reshape(rows, sector)
    zim = z[:, 1].reshape(rows, sector)
    dot = functools.partial(jnp.dot, preferred_element_type=F32)
    re_all = dot(tab[...], jnp.concatenate([zre, -zim], axis=0))
    im_all = dot(tab[...], jnp.concatenate([zim, zre], axis=0))
    ab_count = tab.shape[0] // height
    for ab in range(ab_count):
        span = slice(ab * height, (ab + 1) * height)
        lines = slice(ab * side, (ab + 1) * side)
        cu = cosines[:, lines].T[row : row + height]
        su = sines[:, lines].T[row : row + height]
        for cb in range(cb_count):
            lanes = slice(cb * side, (cb + 1) * side)
            c0, s0 = cu[:, cb : cb + 1], su[:, cb : cb + 1]
            c1 = cosines[cb_count + ab : cb_count + ab + 1, lanes]
            s1 = sines[cb_count + ab : cb_count + ab + 1, lanes]
            cosine = c0 * c1 - s0 * s1
            sine = s0 * c1 + c0 * s1
            r, i = re_all[span, lanes], im_all[span, lanes]
            clean[ab * cb_count + cb, 0] = (r * cosine - i * sine).astype(BF16)
            clean[ab * cb_count + cb, 1] = (r * sine + i * cosine).astype(BF16)
    sums[...] = jnp.zeros_like(sums)
    blocks = ab_count * cb_count
    me = owners[0, blocks]
    chips = own.shape[0]
    for b in range(blocks):
        owner = owners[0, b]
        apart = owner ^ me
        slot = (apart & 1) * chips + ((apart >> 1) & 1) * (chips // 2) + (owner >> 2)
        sums[slot] = (sums[slot].astype(F32) + clean[b].astype(F32)).astype(BF16)
    own[...] = sums[:chips]
    other[...] = sums[chips:]


def focus(part, owners, tab, z, cosines, sines, slots):
    height = BLOCK_SIDE // 2
    vmem = pl.BlockSpec(memory_space=pltpu.VMEM)
    blocks = owners.shape[1] - 1
    operands = [pltpu.with_memory_space_constraint(x, pltpu.VMEM) for x in (tab, z, cosines, sines)]
    shape = pltpu.VMEM((slots // 2, 2, height, BLOCK_SIDE), BF16)
    return pl.pallas_call(
        functools.partial(focus_kernel, part * height),
        out_shape=(shape, shape),
        in_specs=[pl.BlockSpec(memory_space=pltpu.SMEM)] + [vmem] * 4,
        out_specs=(vmem, vmem),
        scratch_shapes=[pltpu.VMEM((n, 2, height, BLOCK_SIDE), BF16) for n in (blocks, slots)],
        name="focus",
    )(owners, *operands)


def on_device(
    dechirped_echo_matrix,
    bearing_rotation_table,
    patch_subset_holder,
    modulation_slope,
    regrid_lead_cell,
    regrid_weight,
):
    groups = lax.axis_size("sub")
    members = lax.axis_size("mem")
    chips = groups // 2
    sector = FREQUENCIES // members
    ab_count = ANGLES // BLOCK_SIDE
    cb_count = sector // BLOCK_SIDE

    by_sector = range_messages(dechirped_echo_matrix[0], members)
    z = lax.all_to_all(by_sector, "mem", split_axis=0, concat_axis=0, tiled=True)

    height = BLOCK_SIDE // 2
    angles = bearing_rotation_table[0, 0].reshape(ab_count, 2, height, SWEEPS)
    tables = [phase_tables(angles[:, part].reshape(ANGLES // 2, SWEEPS)) for part in range(2)]
    positions = jnp.arange(BLOCK_SIDE, dtype=F32)
    slope = modulation_slope[0, 0].reshape(2, ab_count, cb_count)
    u_phase = slope[0].T[:, :, None] * positions
    v_phase = slope[1][:, :, None] * positions
    phase = jnp.concatenate([u_phase, v_phase]).reshape(cb_count + ab_count, sector)
    cosines, sines = jnp.cos(phase), jnp.sin(phase)

    me = lax.axis_index("sub").astype(jnp.int32)
    owners = jnp.concatenate([patch_subset_holder[0], me.reshape(1, 1)], axis=1)
    core_swap = [(i, i ^ 1) for i in range(groups)]

    def pairing(shift):
        partner = lambda z: (((z + shift) ^ 1) - shift) % chips
        return [(2 * z + c, 2 * partner(z) + c) for z in range(chips) for c in range(2)]

    kept = chips // 2
    parts = []
    for part in range(2):
        own, other = focus(part, owners, tables[part], z, cosines, sines, groups)
        held = own + lax.ppermute(other, "sub", core_swap)
        parts.append(held[:kept] + lax.ppermute(held[kept:], "sub", pairing(part)))
    alike = [[2 * z + c for z in range(par, chips, 2)] for par in range(2) for c in range(2)]
    arrived = lax.all_to_all(
        jnp.concatenate(parts, axis=2),
        "sub",
        split_axis=0,
        concat_axis=0,
        tiled=True,
        axis_index_groups=alike,
    )
    gathered = jnp.sum(arrived.astype(F32), axis=0).astype(BF16)
    own_tables = stencil(regrid_lead_cell[0, 0], regrid_weight[0, 0])
    rows_done = jnp.einsum(
        "ya,pac->pyc", own_tables[0], gathered, preferred_element_type=F32
    ).astype(BF16)
    ground = jnp.einsum("pyc,xc->pyx", rows_done, own_tables[1], preferred_element_type=F32)
    return (0.25 * ground).astype(BF16)[None]


def solution(mesh):
    return jax.shard_map(
        on_device,
        mesh=mesh,
        in_specs=(
            P("sub", None, "mem", None),
            P("sub", "mem", None, None),
            P("sub", "mem", None),
            P("sub", "mem", None, None),
            P("sub", "mem", None, None),
            P("sub", "mem", None, None),
        ),
        out_specs=P(("sub", "mem"), None, None, None),
        check_vma=False,
    )
```

```python
import functools
import math

import jax
import jax.numpy as jnp
import numpy as np
from jax import lax
from jax.experimental import pallas as pl
from jax.experimental.pallas import tpu as pltpu
from jax.sharding import PartitionSpec as P

FREQUENCIES = 8192
FIRST_RADIX = 64
SECOND_RADIX = 128
SWEEPS = 256
ANGLES = 512
BLOCK_SIDE = 128
F32 = jnp.float32
BF16 = jnp.bfloat16


def range_constants():
    def table(length, rows):
        turns = np.outer(rows, np.arange(length)) % length
        angle = turns * (2.0 * np.pi / length)
        c, s = np.cos(angle), np.sin(angle)
        return np.concatenate([c, -s], axis=1), np.concatenate([s, c], axis=1)

    first = np.concatenate(table(FIRST_RADIX, np.arange(FIRST_RADIX)))
    second = np.concatenate(
        [part for odd in range(2) for part in table(SECOND_RADIX, np.arange(odd, SECOND_RADIX, 2))]
    )
    turns = np.outer(np.arange(FIRST_RADIX), np.arange(SECOND_RADIX)) % FREQUENCIES
    angle = turns * (2.0 * np.pi / FREQUENCIES)
    return (
        jnp.asarray(first.astype(np.float32)).astype(BF16),
        jnp.asarray(second.astype(np.float32)).astype(BF16),
        jnp.asarray(np.stack([np.cos(angle), np.sin(angle)]).astype(np.float32)),
    )


def range_kernel(x, first, second, turn, out, rows, turned, moved):
    sweeps = x.shape[1]
    lanes = SECOND_RADIX
    height = 2 * FIRST_RADIX
    for p in range(2):
        for k2 in range(FIRST_RADIX):
            tile = x[p, :, k2 * lanes : (k2 + 1) * lanes].astype(F32)
            rows[pl.ds(p * FIRST_RADIX + k2, sweeps, stride=height), :] = tile
    cosine, sine = turn[0], turn[1]
    for s in range(0, sweeps, 2):
        pair = [rows[(s + i) * height : (s + i + 1) * height, :].astype(BF16) for i in range(2)]
        product = jnp.dot(first[...], jnp.concatenate(pair, axis=1), preferred_element_type=F32)
        for i in range(2):
            re = product[:FIRST_RADIX, i * lanes : (i + 1) * lanes]
            im = product[FIRST_RADIX:, i * lanes : (i + 1) * lanes]
            span = slice((s + i) * FIRST_RADIX, (s + i + 1) * FIRST_RADIX)
            turned[span, :lanes] = (re * cosine - im * sine).astype(BF16)
            turned[span, lanes:] = (re * sine + im * cosine).astype(BF16)
    factor = 1.0 / math.sqrt(FREQUENCIES)
    low = lax.broadcasted_iota(jnp.int32, (lanes, lanes), 1) < FIRST_RADIX
    for s in range(0, sweeps, 2):
        span = slice(s * FIRST_RADIX, (s + 2) * FIRST_RADIX)
        product = factor * lax.dot_general(
            second[...], turned[span, :], (((1,), (1,)), ((), ())), preferred_element_type=F32
        )
        even, odd = product[:lanes], product[lanes:]
        here = jnp.where(low, even, pltpu.roll(odd, FIRST_RADIX, 1))
        after = jnp.where(low, pltpu.roll(even, FIRST_RADIX, 1), odd)
        moved[pl.ds(s, lanes, stride=sweeps), :] = here
        moved[pl.ds(s + 1, lanes, stride=sweeps), :] = after
    members = out.shape[0]
    cb_count = out.shape[3] // lanes
    for q in range(2):
        for m in range(members):
            for cb in range(cb_count):
                row = ((q * members + m) * cb_count + cb) * sweeps
                out[m, q, :, cb * lanes : (cb + 1) * lanes] = moved[row : row + sweeps, :].astype(BF16)


def range_messages(sweeps, members):
    count = sweeps.shape[1]
    vmem = pl.BlockSpec(memory_space=pltpu.VMEM)
    return pl.pallas_call(
        range_kernel,
        out_shape=jax.ShapeDtypeStruct((members, 2, count, FREQUENCIES // members), BF16),
        in_specs=[vmem] * 4,
        out_specs=vmem,
        scratch_shapes=[
            pltpu.VMEM((count * 2 * FIRST_RADIX, SECOND_RADIX), F32),
            pltpu.VMEM((count * FIRST_RADIX, 2 * SECOND_RADIX), BF16),
            pltpu.VMEM((count * 2 * FIRST_RADIX, SECOND_RADIX), F32),
        ],
        name="range_transform",
    )(sweeps, *range_constants())


def phase_tables(angles):
    factor = 1.0 / math.sqrt(SWEEPS)
    return jnp.concatenate([jnp.cos(angles) * factor, jnp.sin(angles) * factor], axis=1).astype(BF16)


def stencil(offsets, fractions):
    weights = [
        -fractions * (fractions - 1.0) * (fractions - 2.0) / 6.0,
        (fractions + 1.0) * (fractions - 1.0) * (fractions - 2.0) / 2.0,
        -(fractions + 1.0) * fractions * (fractions - 2.0) / 2.0,
        (fractions + 1.0) * fractions * (fractions - 1.0) / 6.0,
    ]
    sources = jnp.arange(fractions.shape[-1], dtype=jnp.int32)
    distance = sources - offsets[..., None]
    weights_sum = jnp.zeros(distance.shape, F32)
    for stencil_tap in range(4):
        weights_sum = weights_sum + jnp.where(
            distance == stencil_tap, weights[stencil_tap][..., None], F32(0.0)
        )
    return weights_sum.astype(BF16)


def focus_kernel(part, row, owners, tab, z, cosines, sines, own, other, clean, sums):
    side = BLOCK_SIDE
    height = own.shape[2]
    sector = z.shape[-1]
    cb_count = sector // side
    rows = z.shape[0] * z.shape[2]
    zre = z[:, 0].reshape(rows, sector)
    zim = z[:, 1].reshape(rows, sector)
    dot = functools.partial(jnp.dot, preferred_element_type=F32)
    re_all = dot(tab[...], jnp.concatenate([zre, -zim], axis=0))
    im_all = dot(tab[...], jnp.concatenate([zim, zre], axis=0))
    ab_count = tab.shape[0] // height
    for ab in range(ab_count):
        span = slice(ab * height, (ab + 1) * height)
        lines = slice(ab * side, (ab + 1) * side)
        cu = cosines[:, lines].T[row : row + height]
        su = sines[:, lines].T[row : row + height]
        for cb in range(cb_count):
            lanes = slice(cb * side, (cb + 1) * side)
            c0, s0 = cu[:, cb : cb + 1], su[:, cb : cb + 1]
            c1 = cosines[cb_count + ab : cb_count + ab + 1, lanes]
            s1 = sines[cb_count + ab : cb_count + ab + 1, lanes]
            cosine = c0 * c1 - s0 * s1
            sine = s0 * c1 + c0 * s1
            r, i = re_all[span, lanes], im_all[span, lanes]
            clean[ab * cb_count + cb, 0] = (r * cosine - i * sine).astype(BF16)
            clean[ab * cb_count + cb, 1] = (r * sine + i * cosine).astype(BF16)
    sums[...] = jnp.zeros_like(sums)
    blocks = ab_count * cb_count
    me = owners[0, blocks]
    chips = own.shape[0]
    for b in range(blocks):
        owner = owners[0, b]
        apart = owner ^ me
        x = (apart >> 1) & 3
        gray = x ^ (x >> 1)
        order = gray if part else ((gray & 1) << 1) | (x >> 1)
        slot = (apart & 1) * chips + order * (chips // 4) + (owner >> 3)
        sums[slot] = (sums[slot].astype(F32) + clean[b].astype(F32)).astype(BF16)
    own[...] = sums[:chips]
    other[...] = sums[chips:]


def focus(part, owners, tab, z, cosines, sines, slots):
    height = BLOCK_SIDE // 2
    vmem = pl.BlockSpec(memory_space=pltpu.VMEM)
    blocks = owners.shape[1] - 1
    operands = [pltpu.with_memory_space_constraint(x, pltpu.VMEM) for x in (tab, z, cosines, sines)]
    shape = pltpu.VMEM((slots // 2, 2, height, BLOCK_SIDE), BF16)
    return pl.pallas_call(
        functools.partial(focus_kernel, part, part * height),
        out_shape=(shape, shape),
        in_specs=[pl.BlockSpec(memory_space=pltpu.SMEM)] + [vmem] * 4,
        out_specs=(vmem, vmem),
        scratch_shapes=[pltpu.VMEM((n, 2, height, BLOCK_SIDE), BF16) for n in (blocks, slots)],
        name="focus",
    )(owners, *operands)


def on_device(
    dechirped_echo_matrix,
    bearing_rotation_table,
    patch_subset_holder,
    modulation_slope,
    regrid_lead_cell,
    regrid_weight,
):
    groups = lax.axis_size("sub")
    members = lax.axis_size("mem")
    chips = groups // 2
    sector = FREQUENCIES // members
    ab_count = ANGLES // BLOCK_SIDE
    cb_count = sector // BLOCK_SIDE

    by_sector = range_messages(dechirped_echo_matrix[0], members)
    z = lax.all_to_all(by_sector, "mem", split_axis=0, concat_axis=0, tiled=True)

    height = BLOCK_SIDE // 2
    angles = bearing_rotation_table[0, 0].reshape(ab_count, 2, height, SWEEPS)
    tables = [phase_tables(angles[:, part].reshape(ANGLES // 2, SWEEPS)) for part in range(2)]
    positions = jnp.arange(BLOCK_SIDE, dtype=F32)
    slope = modulation_slope[0, 0].reshape(2, ab_count, cb_count)
    u_phase = slope[0].T[:, :, None] * positions
    v_phase = slope[1][:, :, None] * positions
    phase = jnp.concatenate([u_phase, v_phase]).reshape(cb_count + ab_count, sector)
    cosines, sines = jnp.cos(phase), jnp.sin(phase)

    me = lax.axis_index("sub").astype(jnp.int32)
    owners = jnp.concatenate([patch_subset_holder[0], me.reshape(1, 1)], axis=1)
    core_swap = [(i, i ^ 1) for i in range(groups)]

    def pairing(shift):
        partner = lambda z: (((z + shift) ^ 1) - shift) % chips
        return [(2 * z + c, 2 * partner(z) + c) for z in range(chips) for c in range(2)]

    parts = []
    for part in range(2):
        own, other = focus(part, owners, tables[part], z, cosines, sines, groups)
        held = own + lax.ppermute(other, "sub", core_swap)
        for shift in (part, 1 - part):
            kept = held.shape[0] // 2
            held = held[:kept] + lax.ppermute(held[kept:], "sub", pairing(shift))
        parts.append(held)
    alike = [[2 * z + c for z in range(k, chips, 4)] for k in range(4) for c in range(2)]
    arrived = lax.all_to_all(
        jnp.concatenate(parts, axis=2),
        "sub",
        split_axis=0,
        concat_axis=0,
        tiled=True,
        axis_index_groups=alike,
    )
    gathered = jnp.sum(arrived.astype(F32), axis=0).astype(BF16)
    own_tables = stencil(regrid_lead_cell[0, 0], regrid_weight[0, 0])
    rows_done = jnp.einsum(
        "ya,pac->pyc", own_tables[0], gathered, preferred_element_type=F32
    ).astype(BF16)
    ground = jnp.einsum("pyc,xc->pyx", rows_done, own_tables[1], preferred_element_type=F32)
    return (0.25 * ground).astype(BF16)[None]


def solution(mesh):
    return jax.shard_map(
        on_device,
        mesh=mesh,
        in_specs=(
            P("sub", None, "mem", None),
            P("sub", "mem", None, None),
            P("sub", "mem", None),
            P("sub", "mem", None, None),
            P("sub", "mem", None, None),
            P("sub", "mem", None, None),
        ),
        out_specs=P(("sub", "mem"), None, None, None),
        check_vma=False,
    )
```

```python
import functools
import math

import jax
import jax.numpy as jnp
import numpy as np
from jax import lax
from jax.experimental import pallas as pl
from jax.experimental.pallas import tpu as pltpu
from jax.sharding import PartitionSpec as P

FREQUENCIES = 8192
FIRST_RADIX = 64
SECOND_RADIX = 128
SWEEPS = 256
ANGLES = 512
BLOCK_SIDE = 128
PARTS = ((0, 64), (64, 128))
F32 = jnp.float32
BF16 = jnp.bfloat16


def range_constants():
    def table(length, rows):
        turns = np.outer(rows, np.arange(length)) % length
        angle = turns * (2.0 * np.pi / length)
        c, s = np.cos(angle), np.sin(angle)
        return np.concatenate([c, -s], axis=1), np.concatenate([s, c], axis=1)

    first = np.concatenate(table(FIRST_RADIX, np.arange(FIRST_RADIX)))
    second = np.concatenate(
        [part for odd in range(2) for part in table(SECOND_RADIX, np.arange(odd, SECOND_RADIX, 2))]
    )
    turns = np.outer(np.arange(FIRST_RADIX), np.arange(SECOND_RADIX)) % FREQUENCIES
    angle = turns * (2.0 * np.pi / FREQUENCIES)
    return (
        jnp.asarray(first.astype(np.float32)).astype(BF16),
        jnp.asarray(second.astype(np.float32)).astype(BF16),
        jnp.asarray(np.stack([np.cos(angle), np.sin(angle)]).astype(np.float32)),
    )


def range_kernel(x, first, second, turn, out, rows, turned, moved):
    sweeps = x.shape[1]
    lanes = SECOND_RADIX
    height = 2 * FIRST_RADIX
    for p in range(2):
        for k2 in range(FIRST_RADIX):
            tile = x[p, :, k2 * lanes : (k2 + 1) * lanes].astype(F32)
            rows[pl.ds(p * FIRST_RADIX + k2, sweeps, stride=height), :] = tile
    cosine, sine = turn[0], turn[1]
    for s in range(0, sweeps, 2):
        pair = [rows[(s + i) * height : (s + i + 1) * height, :].astype(BF16) for i in range(2)]
        product = jnp.dot(first[...], jnp.concatenate(pair, axis=1), preferred_element_type=F32)
        for i in range(2):
            re = product[:FIRST_RADIX, i * lanes : (i + 1) * lanes]
            im = product[FIRST_RADIX:, i * lanes : (i + 1) * lanes]
            span = slice((s + i) * FIRST_RADIX, (s + i + 1) * FIRST_RADIX)
            turned[span, :lanes] = (re * cosine - im * sine).astype(BF16)
            turned[span, lanes:] = (re * sine + im * cosine).astype(BF16)
    factor = 1.0 / math.sqrt(FREQUENCIES)
    low = lax.broadcasted_iota(jnp.int32, (lanes, lanes), 1) < FIRST_RADIX
    for s in range(0, sweeps, 2):
        span = slice(s * FIRST_RADIX, (s + 2) * FIRST_RADIX)
        product = factor * lax.dot_general(
            second[...], turned[span, :], (((1,), (1,)), ((), ())), preferred_element_type=F32
        )
        even, odd = product[:lanes], product[lanes:]
        here = jnp.where(low, even, pltpu.roll(odd, FIRST_RADIX, 1))
        after = jnp.where(low, pltpu.roll(even, FIRST_RADIX, 1), odd)
        moved[pl.ds(s, lanes, stride=sweeps), :] = here
        moved[pl.ds(s + 1, lanes, stride=sweeps), :] = after
    members = out.shape[0]
    cb_count = out.shape[3] // lanes
    for q in range(2):
        for m in range(members):
            for cb in range(cb_count):
                row = ((q * members + m) * cb_count + cb) * sweeps
                out[m, q, :, cb * lanes : (cb + 1) * lanes] = moved[row : row + sweeps, :].astype(BF16)


def range_messages(sweeps, members):
    count = sweeps.shape[1]
    vmem = pl.BlockSpec(memory_space=pltpu.VMEM)
    return pl.pallas_call(
        range_kernel,
        out_shape=jax.ShapeDtypeStruct((members, 2, count, FREQUENCIES // members), BF16),
        in_specs=[vmem] * 4,
        out_specs=vmem,
        scratch_shapes=[
            pltpu.VMEM((count * 2 * FIRST_RADIX, SECOND_RADIX), F32),
            pltpu.VMEM((count * FIRST_RADIX, 2 * SECOND_RADIX), BF16),
            pltpu.VMEM((count * 2 * FIRST_RADIX, SECOND_RADIX), F32),
        ],
        name="range_transform",
    )(sweeps, *range_constants())


def phase_tables(angles):
    factor = 1.0 / math.sqrt(SWEEPS)
    return jnp.concatenate([jnp.cos(angles) * factor, jnp.sin(angles) * factor], axis=1).astype(BF16)


def stencil(offsets, fractions):
    weights = [
        -fractions * (fractions - 1.0) * (fractions - 2.0) / 6.0,
        (fractions + 1.0) * (fractions - 1.0) * (fractions - 2.0) / 2.0,
        -(fractions + 1.0) * fractions * (fractions - 2.0) / 2.0,
        (fractions + 1.0) * fractions * (fractions - 1.0) / 6.0,
    ]
    sources = jnp.arange(fractions.shape[-1], dtype=jnp.int32)
    distance = sources - offsets[..., None]
    weights_sum = jnp.zeros(distance.shape, F32)
    for stencil_tap in range(4):
        weights_sum = weights_sum + jnp.where(
            distance == stencil_tap, weights[stencil_tap][..., None], F32(0.0)
        )
    return weights_sum.astype(BF16)


def focus_kernel(owners, tab, z, cosines, sines, own, other, clean, sums):
    side = BLOCK_SIDE
    chips = own.shape[0]
    sector = z.shape[-1]
    cb_count = sector // side
    ab_count = tab.shape[0] // side
    rows = z.shape[0] * z.shape[2]
    zre = z[:, 0].reshape(rows, sector)
    zim = z[:, 1].reshape(rows, sector)
    dot = functools.partial(jnp.dot, preferred_element_type=F32)
    re_all = dot(tab[...], jnp.concatenate([zre, -zim], axis=0))
    im_all = dot(tab[...], jnp.concatenate([zim, zre], axis=0))
    for ab in range(ab_count):
        span = slice(ab * side, (ab + 1) * side)
        cu = cosines[:, span].T
        su = sines[:, span].T
        for cb in range(cb_count):
            lanes = slice(cb * side, (cb + 1) * side)
            c0, s0 = cu[:, cb : cb + 1], su[:, cb : cb + 1]
            c1 = cosines[cb_count + ab : cb_count + ab + 1, lanes]
            s1 = sines[cb_count + ab : cb_count + ab + 1, lanes]
            cosine = c0 * c1 - s0 * s1
            sine = s0 * c1 + c0 * s1
            r, i = re_all[span, lanes], im_all[span, lanes]
            clean[ab * cb_count + cb, 0] = (r * cosine - i * sine).astype(BF16)
            clean[ab * cb_count + cb, 1] = (r * sine + i * cosine).astype(BF16)
    sums[...] = jnp.zeros_like(sums)
    blocks = ab_count * cb_count
    me = owners[0, blocks]
    for b in range(blocks):
        owner = owners[0, b]
        apart = owner ^ me
        x = (apart >> 1) & 3
        gray = x ^ (x >> 1)
        for part, order in enumerate((((gray & 1) << 1) | (x >> 1), gray)):
            slot = (apart & 1) * chips + order * (chips // 4) + (owner >> 3)
            lines = slice(*PARTS[part])
            total = sums[slot, :, lines].astype(F32) + clean[b, :, lines].astype(F32)
            sums[slot, :, lines] = total.astype(BF16)
    own[...] = sums[:chips]
    other[...] = sums[chips:]


def focus(owners, tab, z, cosines, sines, slots):
    vmem = pl.BlockSpec(memory_space=pltpu.VMEM)
    blocks = owners.shape[1] - 1
    operands = [pltpu.with_memory_space_constraint(x, pltpu.VMEM) for x in (tab, z, cosines, sines)]
    shape = pltpu.VMEM((slots // 2, 2, BLOCK_SIDE, BLOCK_SIDE), BF16)
    return pl.pallas_call(
        focus_kernel,
        out_shape=(shape, shape),
        in_specs=[pl.BlockSpec(memory_space=pltpu.SMEM)] + [vmem] * 4,
        out_specs=(vmem, vmem),
        scratch_shapes=[
            pltpu.VMEM((n, 2, BLOCK_SIDE, BLOCK_SIDE), BF16) for n in (blocks, slots)
        ],
        compiler_params=pltpu.CompilerParams(vmem_limit_bytes=20 << 20),
        name="focus",
    )(owners, *operands)


def regrid_kernel(arrived, tables, out):
    total = arrived[0].astype(F32)
    for i in range(1, arrived.shape[0]):
        total = total + arrived[i].astype(F32)
    total = total.astype(BF16)
    for p in range(2):
        rows_done = jnp.dot(tables[0], total[p], preferred_element_type=F32).astype(BF16)
        ground = lax.dot_general(
            rows_done, tables[1], (((1,), (1,)), ((), ())), preferred_element_type=F32
        )
        out[p] = (0.25 * ground).astype(BF16)


def regrid(arrived, tables):
    vmem = pl.BlockSpec(memory_space=pltpu.VMEM)
    return pl.pallas_call(
        regrid_kernel,
        out_shape=jax.ShapeDtypeStruct(arrived.shape[1:], BF16),
        in_specs=[vmem] * 2,
        out_specs=vmem,
        compiler_params=pltpu.CompilerParams(vmem_limit_bytes=4 << 20),
        name="regrid",
    )(*(pltpu.with_memory_space_constraint(x, pltpu.VMEM) for x in (arrived, tables)))


def on_device(
    dechirped_echo_matrix,
    bearing_rotation_table,
    patch_subset_holder,
    modulation_slope,
    regrid_lead_cell,
    regrid_weight,
):
    groups = lax.axis_size("sub")
    members = lax.axis_size("mem")
    chips = groups // 2
    sector = FREQUENCIES // members
    ab_count = ANGLES // BLOCK_SIDE
    cb_count = sector // BLOCK_SIDE

    by_sector = range_messages(dechirped_echo_matrix[0], members)
    z = lax.all_to_all(by_sector, "mem", split_axis=0, concat_axis=0, tiled=True)

    tables = phase_tables(bearing_rotation_table[0, 0])
    positions = jnp.arange(BLOCK_SIDE, dtype=F32)
    slope = modulation_slope[0, 0].reshape(2, ab_count, cb_count)
    u_phase = slope[0].T[:, :, None] * positions
    v_phase = slope[1][:, :, None] * positions
    phase = jnp.concatenate([u_phase, v_phase]).reshape(cb_count + ab_count, sector)
    cosines, sines = jnp.cos(phase), jnp.sin(phase)

    me = lax.axis_index("sub").astype(jnp.int32)
    owners = jnp.concatenate([patch_subset_holder[0], me.reshape(1, 1)], axis=1)
    core_swap = [(i, i ^ 1) for i in range(groups)]

    def pairing(shift):
        partner = lambda z: (((z + shift) ^ 1) - shift) % chips
        return [(2 * z + c, 2 * partner(z) + c) for z in range(chips) for c in range(2)]

    own, other = focus(owners, tables, z, cosines, sines, groups)
    arriving = lax.ppermute(other, "sub", core_swap)
    parts = []
    for part in range(2):
        lines = slice(*PARTS[part])
        held = own[:, :, lines] + arriving[:, :, lines]
        for shift in (part, 1 - part):
            kept = held.shape[0] // 2
            held = held[:kept] + lax.ppermute(held[kept:], "sub", pairing(shift))
        parts.append(held)
    alike = [[2 * z + c for z in range(k, chips, 4)] for k in range(4) for c in range(2)]
    arrived = lax.all_to_all(
        jnp.concatenate(parts, axis=2),
        "sub",
        split_axis=0,
        concat_axis=0,
        tiled=True,
        axis_index_groups=alike,
    )
    own_tables = stencil(regrid_lead_cell[0, 0], regrid_weight[0, 0])
    return regrid(arrived, own_tables)[None]


def solution(mesh):
    return jax.shard_map(
        on_device,
        mesh=mesh,
        in_specs=(
            P("sub", None, "mem", None),
            P("sub", "mem", None, None),
            P("sub", "mem", None),
            P("sub", "mem", None, None),
            P("sub", "mem", None, None),
            P("sub", "mem", None, None),
        ),
        out_specs=P(("sub", "mem"), None, None, None),
        check_vma=False,
    )
```

```python
import functools
import math

import jax
import jax.numpy as jnp
import numpy as np
from jax import lax
from jax.experimental import pallas as pl
from jax.experimental.pallas import tpu as pltpu
from jax.sharding import PartitionSpec as P

FREQUENCIES = 8192
FIRST_RADIX = 64
SECOND_RADIX = 128
SWEEPS = 256
ANGLES = 512
BLOCK_SIDE = 128
PARTS = ((0, 64), (64, 128))
F32 = jnp.float32
BF16 = jnp.bfloat16


def range_constants():
    def table(length, rows):
        turns = np.outer(rows, np.arange(length)) % length
        angle = turns * (2.0 * np.pi / length)
        c, s = np.cos(angle), np.sin(angle)
        return np.concatenate([c, -s], axis=1), np.concatenate([s, c], axis=1)

    first = np.concatenate(table(FIRST_RADIX, np.arange(FIRST_RADIX)))
    second = np.concatenate(
        [part for odd in range(2) for part in table(SECOND_RADIX, np.arange(odd, SECOND_RADIX, 2))]
    )
    turns = np.outer(np.arange(FIRST_RADIX), np.arange(SECOND_RADIX)) % FREQUENCIES
    angle = turns * (2.0 * np.pi / FREQUENCIES)
    return (
        jnp.asarray(first.astype(np.float32)).astype(BF16),
        jnp.asarray(second.astype(np.float32)).astype(BF16),
        jnp.asarray(np.stack([np.cos(angle), np.sin(angle)]).astype(np.float32)),
    )


def range_kernel(x, first, second, turn, out, rows, turned, moved):
    sweeps = x.shape[1]
    lanes = SECOND_RADIX
    height = 2 * FIRST_RADIX
    for p in range(2):
        for k2 in range(FIRST_RADIX):
            tile = x[p, :, k2 * lanes : (k2 + 1) * lanes].astype(F32)
            rows[pl.ds(p * FIRST_RADIX + k2, sweeps, stride=height), :] = tile
    cosine, sine = turn[0], turn[1]
    for s in range(0, sweeps, 2):
        pair = [rows[(s + i) * height : (s + i + 1) * height, :].astype(BF16) for i in range(2)]
        product = jnp.dot(first[...], jnp.concatenate(pair, axis=1), preferred_element_type=F32)
        for i in range(2):
            re = product[:FIRST_RADIX, i * lanes : (i + 1) * lanes]
            im = product[FIRST_RADIX:, i * lanes : (i + 1) * lanes]
            span = slice((s + i) * FIRST_RADIX, (s + i + 1) * FIRST_RADIX)
            turned[span, :lanes] = (re * cosine - im * sine).astype(BF16)
            turned[span, lanes:] = (re * sine + im * cosine).astype(BF16)
    factor = 1.0 / math.sqrt(FREQUENCIES)
    low = lax.broadcasted_iota(jnp.int32, (lanes, lanes), 1) < FIRST_RADIX
    for s in range(0, sweeps, 2):
        span = slice(s * FIRST_RADIX, (s + 2) * FIRST_RADIX)
        product = factor * lax.dot_general(
            second[...], turned[span, :], (((1,), (1,)), ((), ())), preferred_element_type=F32
        )
        even, odd = product[:lanes], product[lanes:]
        here = jnp.where(low, even, pltpu.roll(odd, FIRST_RADIX, 1))
        after = jnp.where(low, pltpu.roll(even, FIRST_RADIX, 1), odd)
        moved[pl.ds(s, lanes, stride=sweeps), :] = here
        moved[pl.ds(s + 1, lanes, stride=sweeps), :] = after
    members = out.shape[0]
    cb_count = out.shape[3] // lanes
    for q in range(2):
        for m in range(members):
            for cb in range(cb_count):
                row = ((q * members + m) * cb_count + cb) * sweeps
                out[m, q, :, cb * lanes : (cb + 1) * lanes] = moved[row : row + sweeps, :].astype(BF16)


def range_messages(sweeps, members):
    count = sweeps.shape[1]
    vmem = pl.BlockSpec(memory_space=pltpu.VMEM)
    return pl.pallas_call(
        range_kernel,
        out_shape=jax.ShapeDtypeStruct((members, 2, count, FREQUENCIES // members), BF16),
        in_specs=[vmem] * 4,
        out_specs=vmem,
        scratch_shapes=[
            pltpu.VMEM((count * 2 * FIRST_RADIX, SECOND_RADIX), F32),
            pltpu.VMEM((count * FIRST_RADIX, 2 * SECOND_RADIX), BF16),
            pltpu.VMEM((count * 2 * FIRST_RADIX, SECOND_RADIX), F32),
        ],
        name="range_transform",
    )(sweeps, *range_constants())


def phase_tables(angles):
    factor = 1.0 / math.sqrt(SWEEPS)
    return jnp.concatenate([jnp.cos(angles) * factor, jnp.sin(angles) * factor], axis=1).astype(BF16)


def stencil(offsets, fractions):
    weights = [
        -fractions * (fractions - 1.0) * (fractions - 2.0) / 6.0,
        (fractions + 1.0) * (fractions - 1.0) * (fractions - 2.0) / 2.0,
        -(fractions + 1.0) * fractions * (fractions - 2.0) / 2.0,
        (fractions + 1.0) * fractions * (fractions - 1.0) / 6.0,
    ]
    sources = jnp.arange(fractions.shape[-1], dtype=jnp.int32)
    distance = sources - offsets[..., None]
    weights_sum = jnp.zeros(distance.shape, F32)
    for stencil_tap in range(4):
        weights_sum = weights_sum + jnp.where(
            distance == stencil_tap, weights[stencil_tap][..., None], F32(0.0)
        )
    return weights_sum.astype(BF16)


def focus_kernel(owners, tab, z, cosines, sines, own, other, clean, sums):
    side = BLOCK_SIDE
    chips = own.shape[0]
    sector = z.shape[-1]
    cb_count = sector // side
    ab_count = tab.shape[0] // side
    rows = z.shape[0] * z.shape[2]
    zre = z[:, 0].reshape(rows, sector)
    zim = z[:, 1].reshape(rows, sector)
    dot = functools.partial(jnp.dot, preferred_element_type=F32)
    re_all = dot(tab[...], jnp.concatenate([zre, -zim], axis=0))
    im_all = dot(tab[...], jnp.concatenate([zim, zre], axis=0))
    for ab in range(ab_count):
        span = slice(ab * side, (ab + 1) * side)
        cu = cosines[:, span].T
        su = sines[:, span].T
        for cb in range(cb_count):
            lanes = slice(cb * side, (cb + 1) * side)
            c0, s0 = cu[:, cb : cb + 1], su[:, cb : cb + 1]
            c1 = cosines[cb_count + ab : cb_count + ab + 1, lanes]
            s1 = sines[cb_count + ab : cb_count + ab + 1, lanes]
            cosine = c0 * c1 - s0 * s1
            sine = s0 * c1 + c0 * s1
            r, i = re_all[span, lanes], im_all[span, lanes]
            clean[ab * cb_count + cb, 0] = (r * cosine - i * sine).astype(BF16)
            clean[ab * cb_count + cb, 1] = (r * sine + i * cosine).astype(BF16)
    sums[...] = jnp.zeros_like(sums)
    blocks = ab_count * cb_count
    me = owners[0, blocks]
    for b in range(blocks):
        owner = owners[0, b]
        apart = owner ^ me
        x = (apart >> 1) & 3
        gray = x ^ (x >> 1)
        for part, order in enumerate((((gray & 1) << 1) | (x >> 1), gray)):
            slot = (apart & 1) * chips + order * (chips // 4) + (owner >> 3)
            lines = slice(*PARTS[part])
            total = sums[slot, :, lines].astype(F32) + clean[b, :, lines].astype(F32)
            sums[slot, :, lines] = total.astype(BF16)
    own[...] = sums[:chips]
    other[...] = sums[chips:]


def focus(owners, tab, z, cosines, sines, slots):
    vmem = pl.BlockSpec(memory_space=pltpu.VMEM)
    blocks = owners.shape[1] - 1
    operands = [pltpu.with_memory_space_constraint(x, pltpu.VMEM) for x in (tab, z, cosines, sines)]
    shape = pltpu.VMEM((slots // 2, 2, BLOCK_SIDE, BLOCK_SIDE), BF16)
    return pl.pallas_call(
        focus_kernel,
        out_shape=(shape, shape),
        in_specs=[pl.BlockSpec(memory_space=pltpu.SMEM)] + [vmem] * 4,
        out_specs=(vmem, vmem),
        scratch_shapes=[
            pltpu.VMEM((n, 2, BLOCK_SIDE, BLOCK_SIDE), BF16) for n in (blocks, slots)
        ],
        compiler_params=pltpu.CompilerParams(vmem_limit_bytes=20 << 20),
        name="focus",
    )(owners, *operands)


def regrid_kernel(*refs):
    *arrived, tables, out = refs
    total = arrived[0][...].astype(F32)
    for part in arrived[1:]:
        total = total + part[...].astype(F32)
    total = total.astype(BF16)
    for p in range(2):
        rows_done = jnp.dot(tables[0], total[p], preferred_element_type=F32).astype(BF16)
        ground = lax.dot_general(
            rows_done, tables[1], (((1,), (1,)), ((), ())), preferred_element_type=F32
        )
        out[p] = (0.25 * ground).astype(BF16)


def regrid(arrived, tables):
    vmem = pl.BlockSpec(memory_space=pltpu.VMEM)
    return pl.pallas_call(
        regrid_kernel,
        out_shape=jax.ShapeDtypeStruct(arrived[0].shape, BF16),
        in_specs=[vmem] * (len(arrived) + 1),
        out_specs=vmem,
        compiler_params=pltpu.CompilerParams(vmem_limit_bytes=4 << 20),
        name="regrid",
    )(*(pltpu.with_memory_space_constraint(x, pltpu.VMEM) for x in (*arrived, tables)))


def on_device(
    dechirped_echo_matrix,
    bearing_rotation_table,
    patch_subset_holder,
    modulation_slope,
    regrid_lead_cell,
    regrid_weight,
):
    groups = lax.axis_size("sub")
    members = lax.axis_size("mem")
    chips = groups // 2
    sector = FREQUENCIES // members
    ab_count = ANGLES // BLOCK_SIDE
    cb_count = sector // BLOCK_SIDE

    by_sector = range_messages(dechirped_echo_matrix[0], members)
    z = lax.all_to_all(by_sector, "mem", split_axis=0, concat_axis=0, tiled=True)

    tables = phase_tables(bearing_rotation_table[0, 0])
    positions = jnp.arange(BLOCK_SIDE, dtype=F32)
    slope = modulation_slope[0, 0].reshape(2, ab_count, cb_count)
    u_phase = slope[0].T[:, :, None] * positions
    v_phase = slope[1][:, :, None] * positions
    phase = jnp.concatenate([u_phase, v_phase]).reshape(cb_count + ab_count, sector)
    cosines, sines = jnp.cos(phase), jnp.sin(phase)

    me = lax.axis_index("sub").astype(jnp.int32)
    owners = jnp.concatenate([patch_subset_holder[0], me.reshape(1, 1)], axis=1)
    core_swap = [(i, i ^ 1) for i in range(groups)]

    def pairing(shift):
        partner = lambda z: (((z + shift) ^ 1) - shift) % chips
        return [(2 * z + c, 2 * partner(z) + c) for z in range(chips) for c in range(2)]

    own, other = focus(owners, tables, z, cosines, sines, groups)
    arriving = lax.ppermute(other, "sub", core_swap)
    parts = []
    for part in range(2):
        lines = slice(*PARTS[part])
        held = own[:, :, lines] + arriving[:, :, lines]
        for shift in (part, 1 - part):
            kept = held.shape[0] // 2
            held = held[:kept] + lax.ppermute(held[kept:], "sub", pairing(shift))
        parts.append(held)
    held = jnp.concatenate(parts, axis=2)
    quarter = me >> 3
    chunk = lambda k: lax.dynamic_index_in_dim(held, (quarter + k) & 3, 0, keepdims=False)
    along = lambda k: [(i, (i + 8 * k) % groups) for i in range(groups)]
    arrived = [lax.ppermute(chunk(k), "sub", along(k)) for k in (2, 1, 3)] + [chunk(0)]
    own_tables = stencil(regrid_lead_cell[0, 0], regrid_weight[0, 0])
    return regrid(arrived, own_tables)[None]


def solution(mesh):
    return jax.shard_map(
        on_device,
        mesh=mesh,
        in_specs=(
            P("sub", None, "mem", None),
            P("sub", "mem", None, None),
            P("sub", "mem", None),
            P("sub", "mem", None, None),
            P("sub", "mem", None, None),
            P("sub", "mem", None, None),
        ),
        out_specs=P(("sub", "mem"), None, None, None),
        check_vma=False,
    )
```

```python
import functools
import math

import jax
import jax.numpy as jnp
import numpy as np
from jax import lax
from jax.experimental import pallas as pl
from jax.experimental.pallas import tpu as pltpu
from jax.sharding import PartitionSpec as P

FREQUENCIES = 8192
FIRST_RADIX = 64
SECOND_RADIX = 128
SWEEPS = 256
ANGLES = 512
BLOCK_SIDE = 128
PARTS = ((0, 64), (64, 128))
F32 = jnp.float32
BF16 = jnp.bfloat16


def range_constants():
    def table(length, rows):
        turns = np.outer(rows, np.arange(length)) % length
        angle = turns * (2.0 * np.pi / length)
        c, s = np.cos(angle), np.sin(angle)
        return np.concatenate([c, -s], axis=1), np.concatenate([s, c], axis=1)

    first = np.concatenate(table(FIRST_RADIX, np.arange(FIRST_RADIX)))
    second = np.concatenate(
        [part for odd in range(2) for part in table(SECOND_RADIX, np.arange(odd, SECOND_RADIX, 2))]
    )
    turns = np.outer(np.arange(FIRST_RADIX), np.arange(SECOND_RADIX)) % FREQUENCIES
    angle = turns * (2.0 * np.pi / FREQUENCIES)
    return (
        jnp.asarray(first.astype(np.float32)).astype(BF16),
        jnp.asarray(second.astype(np.float32)).astype(BF16),
        jnp.asarray(np.stack([np.cos(angle), np.sin(angle)]).astype(np.float32)),
    )


def range_kernel(x, first, second, turn, out, rows, turned, moved):
    sweeps = x.shape[1]
    lanes = SECOND_RADIX
    height = 2 * FIRST_RADIX
    for p in range(2):
        for k2 in range(FIRST_RADIX):
            tile = x[p, :, k2 * lanes : (k2 + 1) * lanes].astype(F32)
            rows[pl.ds(p * FIRST_RADIX + k2, sweeps, stride=height), :] = tile
    cosine, sine = turn[0], turn[1]
    for s in range(0, sweeps, 2):
        pair = [rows[(s + i) * height : (s + i + 1) * height, :].astype(BF16) for i in range(2)]
        product = jnp.dot(first[...], jnp.concatenate(pair, axis=1), preferred_element_type=F32)
        for i in range(2):
            re = product[:FIRST_RADIX, i * lanes : (i + 1) * lanes]
            im = product[FIRST_RADIX:, i * lanes : (i + 1) * lanes]
            span = slice((s + i) * FIRST_RADIX, (s + i + 1) * FIRST_RADIX)
            turned[span, :lanes] = (re * cosine - im * sine).astype(BF16)
            turned[span, lanes:] = (re * sine + im * cosine).astype(BF16)
    factor = 1.0 / math.sqrt(FREQUENCIES)
    low = lax.broadcasted_iota(jnp.int32, (lanes, lanes), 1) < FIRST_RADIX
    for s in range(0, sweeps, 2):
        span = slice(s * FIRST_RADIX, (s + 2) * FIRST_RADIX)
        product = factor * lax.dot_general(
            second[...], turned[span, :], (((1,), (1,)), ((), ())), preferred_element_type=F32
        )
        even, odd = product[:lanes], product[lanes:]
        here = jnp.where(low, even, pltpu.roll(odd, FIRST_RADIX, 1))
        after = jnp.where(low, pltpu.roll(even, FIRST_RADIX, 1), odd)
        moved[pl.ds(s, lanes, stride=sweeps), :] = here
        moved[pl.ds(s + 1, lanes, stride=sweeps), :] = after
    members = out.shape[0]
    cb_count = out.shape[3] // lanes
    for q in range(2):
        for m in range(members):
            for cb in range(cb_count):
                row = ((q * members + m) * cb_count + cb) * sweeps
                out[m, q, :, cb * lanes : (cb + 1) * lanes] = moved[row : row + sweeps, :].astype(BF16)


def range_messages(sweeps, members):
    count = sweeps.shape[1]
    vmem = pl.BlockSpec(memory_space=pltpu.VMEM)
    return pl.pallas_call(
        range_kernel,
        out_shape=jax.ShapeDtypeStruct((members, 2, count, FREQUENCIES // members), BF16),
        in_specs=[vmem] * 4,
        out_specs=vmem,
        scratch_shapes=[
            pltpu.VMEM((count * 2 * FIRST_RADIX, SECOND_RADIX), F32),
            pltpu.VMEM((count * FIRST_RADIX, 2 * SECOND_RADIX), BF16),
            pltpu.VMEM((count * 2 * FIRST_RADIX, SECOND_RADIX), F32),
        ],
        name="range_transform",
    )(sweeps, *range_constants())


def phase_tables(angles):
    factor = 1.0 / math.sqrt(SWEEPS)
    return jnp.concatenate([jnp.cos(angles) * factor, jnp.sin(angles) * factor], axis=1).astype(BF16)


def stencil(offsets, fractions):
    weights = [
        -fractions * (fractions - 1.0) * (fractions - 2.0) / 6.0,
        (fractions + 1.0) * (fractions - 1.0) * (fractions - 2.0) / 2.0,
        -(fractions + 1.0) * fractions * (fractions - 2.0) / 2.0,
        (fractions + 1.0) * fractions * (fractions - 1.0) / 6.0,
    ]
    sources = jnp.arange(fractions.shape[-1], dtype=jnp.int32)
    distance = sources - offsets[..., None]
    weights_sum = jnp.zeros(distance.shape, F32)
    for stencil_tap in range(4):
        weights_sum = weights_sum + jnp.where(
            distance == stencil_tap, weights[stencil_tap][..., None], F32(0.0)
        )
    return weights_sum.astype(BF16)


def focus_kernel(owners, tab, z, cosines, sines, own, other, clean, sums):
    side = BLOCK_SIDE
    chips = own.shape[0]
    sector = z.shape[-1]
    cb_count = sector // side
    ab_count = tab.shape[0] // side
    rows = z.shape[0] * z.shape[2]
    zre = z[:, 0].reshape(rows, sector)
    zim = z[:, 1].reshape(rows, sector)
    dot = functools.partial(jnp.dot, preferred_element_type=F32)
    re_all = dot(tab[...], jnp.concatenate([zre, -zim], axis=0))
    im_all = dot(tab[...], jnp.concatenate([zim, zre], axis=0))
    for ab in range(ab_count):
        span = slice(ab * side, (ab + 1) * side)
        cu = cosines[:, span].T
        su = sines[:, span].T
        for cb in range(cb_count):
            lanes = slice(cb * side, (cb + 1) * side)
            c0, s0 = cu[:, cb : cb + 1], su[:, cb : cb + 1]
            c1 = cosines[cb_count + ab : cb_count + ab + 1, lanes]
            s1 = sines[cb_count + ab : cb_count + ab + 1, lanes]
            cosine = c0 * c1 - s0 * s1
            sine = s0 * c1 + c0 * s1
            r, i = re_all[span, lanes], im_all[span, lanes]
            clean[ab * cb_count + cb, 0] = (r * cosine - i * sine).astype(BF16)
            clean[ab * cb_count + cb, 1] = (r * sine + i * cosine).astype(BF16)
    sums[...] = jnp.zeros_like(sums)
    blocks = ab_count * cb_count
    me = owners[0, blocks]
    for b in range(blocks):
        owner = owners[0, b]
        apart = owner ^ me
        x = (apart >> 1) & 3
        gray = x ^ (x >> 1)
        for part, order in enumerate((((gray & 1) << 1) | (x >> 1), gray)):
            slot = (apart & 1) * chips + order * (chips // 4) + (owner >> 3)
            lines = slice(*PARTS[part])
            total = sums[slot, :, lines].astype(F32) + clean[b, :, lines].astype(F32)
            sums[slot, :, lines] = total.astype(BF16)
    own[...] = sums[:chips]
    other[...] = sums[chips:]


def focus(owners, tab, z, cosines, sines, slots):
    vmem = pl.BlockSpec(memory_space=pltpu.VMEM)
    blocks = owners.shape[1] - 1
    operands = [pltpu.with_memory_space_constraint(x, pltpu.VMEM) for x in (tab, z, cosines, sines)]
    shape = pltpu.VMEM((slots // 2, 2, BLOCK_SIDE, BLOCK_SIDE), BF16)
    return pl.pallas_call(
        focus_kernel,
        out_shape=(shape, shape),
        in_specs=[pl.BlockSpec(memory_space=pltpu.SMEM)] + [vmem] * 4,
        out_specs=(vmem, vmem),
        scratch_shapes=[
            pltpu.VMEM((n, 2, BLOCK_SIDE, BLOCK_SIDE), BF16) for n in (blocks, slots)
        ],
        compiler_params=pltpu.CompilerParams(vmem_limit_bytes=20 << 20),
        name="focus",
    )(owners, *operands)


def regrid_kernel(*refs):
    *arrived, tables, out = refs
    total = arrived[0][...].astype(F32)
    for part in arrived[1:]:
        total = total + part[...].astype(F32)
    total = total.astype(BF16)
    for p in range(2):
        rows_done = jnp.dot(tables[0], total[p], preferred_element_type=F32).astype(BF16)
        ground = lax.dot_general(
            rows_done, tables[1], (((1,), (1,)), ((), ())), preferred_element_type=F32
        )
        out[p] = (0.25 * ground).astype(BF16)


def regrid(arrived, tables):
    vmem = pl.BlockSpec(memory_space=pltpu.VMEM)
    return pl.pallas_call(
        regrid_kernel,
        out_shape=jax.ShapeDtypeStruct(arrived[0].shape, BF16),
        in_specs=[vmem] * (len(arrived) + 1),
        out_specs=vmem,
        compiler_params=pltpu.CompilerParams(vmem_limit_bytes=4 << 20),
        name="regrid",
    )(*(pltpu.with_memory_space_constraint(x, pltpu.VMEM) for x in (*arrived, tables)))


def on_device(
    dechirped_echo_matrix,
    bearing_rotation_table,
    patch_subset_holder,
    modulation_slope,
    regrid_lead_cell,
    regrid_weight,
):
    groups = lax.axis_size("sub")
    members = lax.axis_size("mem")
    chips = groups // 2
    sector = FREQUENCIES // members
    ab_count = ANGLES // BLOCK_SIDE
    cb_count = sector // BLOCK_SIDE

    by_sector = range_messages(dechirped_echo_matrix[0], members)
    z = lax.all_to_all(by_sector, "mem", split_axis=0, concat_axis=0, tiled=True)

    tables = phase_tables(bearing_rotation_table[0, 0])
    positions = jnp.arange(BLOCK_SIDE, dtype=F32)
    slope = modulation_slope[0, 0].reshape(2, ab_count, cb_count)
    u_phase = slope[0].T[:, :, None] * positions
    v_phase = slope[1][:, :, None] * positions
    phase = jnp.concatenate([u_phase, v_phase]).reshape(cb_count + ab_count, sector)
    cosines, sines = jnp.cos(phase), jnp.sin(phase)

    me = lax.axis_index("sub").astype(jnp.int32)
    owners = jnp.concatenate([patch_subset_holder[0], me.reshape(1, 1)], axis=1)
    core_swap = [(i, i ^ 1) for i in range(groups)]

    def pairing(shift):
        partner = lambda z: (((z + shift) ^ 1) - shift) % chips
        return [(2 * z + c, 2 * partner(z) + c) for z in range(chips) for c in range(2)]

    own, other = focus(owners, tables, z, cosines, sines, groups)
    arriving = lax.ppermute(other, "sub", core_swap)
    parts = []
    for part in range(2):
        lines = slice(*PARTS[part])
        held = own[:, :, lines] + arriving[:, :, lines]
        for shift in (part, 1 - part):
            kept = held.shape[0] // 2
            held = held[:kept] + lax.ppermute(held[kept:], "sub", pairing(shift))
        parts.append(held)
    held = jnp.concatenate(parts, axis=2)
    quarter = me >> 3
    chunk = lambda k: lax.dynamic_index_in_dim(held, (quarter + k) & 3, 0, keepdims=False)
    along = lambda k: [(i, (i + 8 * k) % groups) for i in range(groups)]
    arrived = [lax.ppermute(chunk(k), "sub", along(k)) for k in (2, 3, 1)] + [chunk(0)]
    own_tables = stencil(regrid_lead_cell[0, 0], regrid_weight[0, 0])
    return regrid(arrived, own_tables)[None]


def solution(mesh):
    return jax.shard_map(
        on_device,
        mesh=mesh,
        in_specs=(
            P("sub", None, "mem", None),
            P("sub", "mem", None, None),
            P("sub", "mem", None),
            P("sub", "mem", None, None),
            P("sub", "mem", None, None),
            P("sub", "mem", None, None),
        ),
        out_specs=P(("sub", "mem"), None, None, None),
        check_vma=False,
    )
```

```python
import functools
import math

import jax
import jax.numpy as jnp
import numpy as np
from jax import lax
from jax.experimental import pallas as pl
from jax.experimental.pallas import tpu as pltpu
from jax.sharding import PartitionSpec as P

FREQUENCIES = 8192
FIRST_RADIX = 64
SECOND_RADIX = 128
SWEEPS = 256
ANGLES = 512
BLOCK_SIDE = 128
PARTS = ((0, 64), (64, 128))
F32 = jnp.float32
BF16 = jnp.bfloat16


def range_constants():
    def table(length, rows):
        turns = np.outer(rows, np.arange(length)) % length
        angle = turns * (2.0 * np.pi / length)
        c, s = np.cos(angle), np.sin(angle)
        return np.concatenate([c, -s], axis=1), np.concatenate([s, c], axis=1)

    first = np.concatenate(table(FIRST_RADIX, np.arange(FIRST_RADIX)))
    second = np.concatenate(
        [part for odd in range(2) for part in table(SECOND_RADIX, np.arange(odd, SECOND_RADIX, 2))]
    )
    turns = np.outer(np.arange(FIRST_RADIX), np.arange(SECOND_RADIX)) % FREQUENCIES
    angle = turns * (2.0 * np.pi / FREQUENCIES)
    return (
        jnp.asarray(first.astype(np.float32)).astype(BF16),
        jnp.asarray(second.astype(np.float32)).astype(BF16),
        jnp.asarray(np.stack([np.cos(angle), np.sin(angle)]).astype(np.float32)),
    )


def range_kernel(x, first, second, turn, out, rows, turned, moved):
    sweeps = x.shape[1]
    lanes = SECOND_RADIX
    height = 2 * FIRST_RADIX
    for p in range(2):
        for k2 in range(FIRST_RADIX):
            tile = x[p, :, k2 * lanes : (k2 + 1) * lanes].astype(F32)
            rows[pl.ds(p * FIRST_RADIX + k2, sweeps, stride=height), :] = tile
    cosine, sine = turn[0], turn[1]
    for s in range(0, sweeps, 2):
        pair = [rows[(s + i) * height : (s + i + 1) * height, :].astype(BF16) for i in range(2)]
        product = jnp.dot(first[...], jnp.concatenate(pair, axis=1), preferred_element_type=F32)
        for i in range(2):
            re = product[:FIRST_RADIX, i * lanes : (i + 1) * lanes]
            im = product[FIRST_RADIX:, i * lanes : (i + 1) * lanes]
            span = slice((s + i) * FIRST_RADIX, (s + i + 1) * FIRST_RADIX)
            turned[span, :lanes] = (re * cosine - im * sine).astype(BF16)
            turned[span, lanes:] = (re * sine + im * cosine).astype(BF16)
    factor = 1.0 / math.sqrt(FREQUENCIES)
    low = lax.broadcasted_iota(jnp.int32, (lanes, lanes), 1) < FIRST_RADIX
    for s in range(0, sweeps, 2):
        span = slice(s * FIRST_RADIX, (s + 2) * FIRST_RADIX)
        product = factor * lax.dot_general(
            second[...], turned[span, :], (((1,), (1,)), ((), ())), preferred_element_type=F32
        )
        even, odd = product[:lanes], product[lanes:]
        here = jnp.where(low, even, pltpu.roll(odd, FIRST_RADIX, 1))
        after = jnp.where(low, pltpu.roll(even, FIRST_RADIX, 1), odd)
        moved[pl.ds(s, lanes, stride=sweeps), :] = here
        moved[pl.ds(s + 1, lanes, stride=sweeps), :] = after
    members = out.shape[0]
    cb_count = out.shape[3] // lanes
    for q in range(2):
        for m in range(members):
            for cb in range(cb_count):
                row = ((q * members + m) * cb_count + cb) * sweeps
                out[m, q, :, cb * lanes : (cb + 1) * lanes] = moved[row : row + sweeps, :].astype(BF16)


def range_messages(sweeps, members):
    count = sweeps.shape[1]
    vmem = pl.BlockSpec(memory_space=pltpu.VMEM)
    return pl.pallas_call(
        range_kernel,
        out_shape=jax.ShapeDtypeStruct((members, 2, count, FREQUENCIES // members), BF16),
        in_specs=[vmem] * 4,
        out_specs=vmem,
        scratch_shapes=[
            pltpu.VMEM((count * 2 * FIRST_RADIX, SECOND_RADIX), F32),
            pltpu.VMEM((count * FIRST_RADIX, 2 * SECOND_RADIX), BF16),
            pltpu.VMEM((count * 2 * FIRST_RADIX, SECOND_RADIX), F32),
        ],
        name="range_transform",
    )(sweeps, *range_constants())


def phase_tables(angles):
    factor = 1.0 / math.sqrt(SWEEPS)
    return jnp.concatenate([jnp.cos(angles) * factor, jnp.sin(angles) * factor], axis=1).astype(BF16)


def stencil(offsets, fractions):
    weights = [
        -fractions * (fractions - 1.0) * (fractions - 2.0) / 6.0,
        (fractions + 1.0) * (fractions - 1.0) * (fractions - 2.0) / 2.0,
        -(fractions + 1.0) * fractions * (fractions - 2.0) / 2.0,
        (fractions + 1.0) * fractions * (fractions - 1.0) / 6.0,
    ]
    sources = jnp.arange(fractions.shape[-1], dtype=jnp.int32)
    distance = sources - offsets[..., None]
    weights_sum = jnp.zeros(distance.shape, F32)
    for stencil_tap in range(4):
        weights_sum = weights_sum + jnp.where(
            distance == stencil_tap, weights[stencil_tap][..., None], F32(0.0)
        )
    return weights_sum.astype(BF16)


def focus_kernel(owners, tab, z, cosines, sines, own, other, clean, sums):
    side = BLOCK_SIDE
    chips = own.shape[0]
    sector = z.shape[-1]
    cb_count = sector // side
    ab_count = tab.shape[0] // side
    rows = z.shape[0] * z.shape[2]
    zre = z[:, 0].reshape(rows, sector)
    zim = z[:, 1].reshape(rows, sector)
    dot = functools.partial(jnp.dot, preferred_element_type=F32)
    re_all = dot(tab[...], jnp.concatenate([zre, -zim], axis=0))
    im_all = dot(tab[...], jnp.concatenate([zim, zre], axis=0))
    for ab in range(ab_count):
        span = slice(ab * side, (ab + 1) * side)
        cu = cosines[:, span].T
        su = sines[:, span].T
        for cb in range(cb_count):
            lanes = slice(cb * side, (cb + 1) * side)
            c0, s0 = cu[:, cb : cb + 1], su[:, cb : cb + 1]
            c1 = cosines[cb_count + ab : cb_count + ab + 1, lanes]
            s1 = sines[cb_count + ab : cb_count + ab + 1, lanes]
            cosine = c0 * c1 - s0 * s1
            sine = s0 * c1 + c0 * s1
            r, i = re_all[span, lanes], im_all[span, lanes]
            clean[ab * cb_count + cb, 0] = (r * cosine - i * sine).astype(BF16)
            clean[ab * cb_count + cb, 1] = (r * sine + i * cosine).astype(BF16)
    sums[...] = jnp.zeros_like(sums)
    blocks = ab_count * cb_count
    me = owners[0, blocks]
    for b in range(blocks):
        owner = owners[0, b]
        apart = owner ^ me
        x = (apart >> 1) & 3
        gray = x ^ (x >> 1)
        for part, order in enumerate((((gray & 1) << 1) | (x >> 1), gray)):
            slot = (apart & 1) * chips + order * (chips // 4) + (owner >> 3)
            lines = slice(*PARTS[part])
            total = sums[slot, :, lines].astype(F32) + clean[b, :, lines].astype(F32)
            sums[slot, :, lines] = total.astype(BF16)
    own[...] = sums[:chips]
    other[...] = sums[chips:]


def focus(owners, tab, z, cosines, sines, slots):
    vmem = pl.BlockSpec(memory_space=pltpu.VMEM)
    blocks = owners.shape[1] - 1
    operands = [pltpu.with_memory_space_constraint(x, pltpu.VMEM) for x in (tab, z, cosines, sines)]
    shape = pltpu.VMEM((slots // 2, 2, BLOCK_SIDE, BLOCK_SIDE), BF16)
    return pl.pallas_call(
        focus_kernel,
        out_shape=(shape, shape),
        in_specs=[pl.BlockSpec(memory_space=pltpu.SMEM)] + [vmem] * 4,
        out_specs=(vmem, vmem),
        scratch_shapes=[
            pltpu.VMEM((n, 2, BLOCK_SIDE, BLOCK_SIDE), BF16) for n in (blocks, slots)
        ],
        compiler_params=pltpu.CompilerParams(vmem_limit_bytes=20 << 20),
        name="focus",
    )(owners, *operands)


def regrid_kernel(*refs):
    *arrived, tables, out = refs
    total = arrived[0][...].astype(F32)
    for part in arrived[1:]:
        total = total + part[...].astype(F32)
    total = total.astype(BF16)
    for p in range(2):
        rows_done = jnp.dot(tables[0], total[p], preferred_element_type=F32).astype(BF16)
        ground = lax.dot_general(
            rows_done, tables[1], (((1,), (1,)), ((), ())), preferred_element_type=F32
        )
        out[p] = (0.25 * ground).astype(BF16)


def regrid(arrived, tables):
    vmem = pl.BlockSpec(memory_space=pltpu.VMEM)
    return pl.pallas_call(
        regrid_kernel,
        out_shape=jax.ShapeDtypeStruct(arrived[0].shape, BF16),
        in_specs=[vmem] * (len(arrived) + 1),
        out_specs=vmem,
        compiler_params=pltpu.CompilerParams(vmem_limit_bytes=4 << 20),
        name="regrid",
    )(*(pltpu.with_memory_space_constraint(x, pltpu.VMEM) for x in (*arrived, tables)))


def on_device(
    dechirped_echo_matrix,
    bearing_rotation_table,
    patch_subset_holder,
    modulation_slope,
    regrid_lead_cell,
    regrid_weight,
):
    groups = lax.axis_size("sub")
    members = lax.axis_size("mem")
    chips = groups // 2
    sector = FREQUENCIES // members
    ab_count = ANGLES // BLOCK_SIDE
    cb_count = sector // BLOCK_SIDE

    by_sector = range_messages(dechirped_echo_matrix[0], members)
    z = lax.all_to_all(by_sector, "mem", split_axis=0, concat_axis=0, tiled=True)

    tables = phase_tables(bearing_rotation_table[0, 0])
    positions = jnp.arange(BLOCK_SIDE, dtype=F32)
    slope = modulation_slope[0, 0].reshape(2, ab_count, cb_count)
    u_phase = slope[0].T[:, :, None] * positions
    v_phase = slope[1][:, :, None] * positions
    phase = jnp.concatenate([u_phase, v_phase]).reshape(cb_count + ab_count, sector)
    cosines, sines = jnp.cos(phase), jnp.sin(phase)

    me = lax.axis_index("sub").astype(jnp.int32)
    owners = jnp.concatenate([patch_subset_holder[0], me.reshape(1, 1)], axis=1)
    core_swap = [(i, i ^ 1) for i in range(groups)]

    def pairing(shift):
        partner = lambda z: (((z + shift) ^ 1) - shift) % chips
        return [(2 * z + c, 2 * partner(z) + c) for z in range(chips) for c in range(2)]

    own, other = focus(owners, tables, z, cosines, sines, groups)
    arriving = lax.ppermute(other, "sub", core_swap)
    parts = []
    for part in range(2):
        lines = slice(*PARTS[part])
        held = own[:, :, lines] + arriving[:, :, lines]
        for shift in (part, 1 - part):
            kept = held.shape[0] // 2
            held = held[:kept] + lax.ppermute(held[kept:], "sub", pairing(shift))
        parts.append(held)
    held = jnp.concatenate(parts, axis=2)
    quarter = me >> 3
    chunk = lambda k: lax.dynamic_index_in_dim(held, (quarter + k) & 3, 0, keepdims=False)
    along = lambda k: [(i, (i + 8 * k) % groups) for i in range(groups)]
    arrived = [lax.ppermute(chunk(k), "sub", along(k)) for k in (3, 2, 1)] + [chunk(0)]
    own_tables = stencil(regrid_lead_cell[0, 0], regrid_weight[0, 0])
    return regrid(arrived, own_tables)[None]


def solution(mesh):
    return jax.shard_map(
        on_device,
        mesh=mesh,
        in_specs=(
            P("sub", None, "mem", None),
            P("sub", "mem", None, None),
            P("sub", "mem", None),
            P("sub", "mem", None, None),
            P("sub", "mem", None, None),
            P("sub", "mem", None, None),
        ),
        out_specs=P(("sub", "mem"), None, None, None),
        check_vma=False,
    )
```
